256 devices in a mesh: grp: 2 (over x_lo), ty: 4 (over x_hi, core), tx: 32 (over y, z).
Axes of the slice: x: 4 (x_hi: 2, x_lo: 2; x = x_hi * 2 + x_lo), y: 4, z: 8, core: 2. Of those that a mesh axis runs over, the one named last changes fastest.
Arguments:
- adjoint_state: float32 [2, 5, 50, 384, 1536], P('grp', None, None, 'tx', 'ty'), may hold values from -6 to 6
- land_mask: int32 [2, 384, 1536], P('grp', 'tx', 'ty'), may hold values 0 or 1
- diffusivity: float32 [2, 384, 1536], P('grp', 'tx', 'ty'), may hold values from 0.02 to 0.24
- mixing: float32 [2, 5, 50, 50], P('grp'), may hold values from -0.875 to 0.875
- nudging: float32 [384, 1536], P('tx', 'ty'), may hold values from 0.1 to 1
- nest_x: int32 [128], P(('ty', 'tx')), may hold values from 0 to 8
- nest_y: int32 [128], P(('ty', 'tx')), may hold values from 0 to 256
- obs_forcing: float32 [2, 128, 16, 128], P('grp', ('ty', 'tx')), may hold values from -6 to 6
- obs_cell: int32 [2, 128, 16, 128], P('grp', None, None, ('ty', 'tx')), may hold values from 0 to 1151999
- obs_count: int32 [2, 128, 128], P('grp', None, ('ty', 'tx')), may hold values from 0 to 16, as said below
Outputs:
- updated_state: float32 [2, 5, 50, 384, 1536], P('grp', None, None, 'tx', 'ty')
The draws below stay inside these ranges and needn't reach their ends.
Inputs may be any that keep to these rules, and one draw needn't show every extreme that they name: `obs_count`: in every draw some destination tile of each grid receives 16 live slots from every source tile; which one is drawn.
All inputs are finite; a program needn't handle non-finite values. No bound on the sum of `land_mask` on one device may be relied on, other than what follows from the above.
Results may differ from the reference program's by a relative error of at most 0.0003.
Values sent between devices are 32-bit elements; how exact they have to be, the bound alone decides.
A program may use at most 128 MiB of HBM per device.

```python
import math
import jax
import jax.numpy as jnp
from jax import lax

F = 5
L = 50
CX = 12
CY = 384
SLOT = 16
NT = 128
NX = 384
NY = 1536


def draw_obs_count(key, part):
    first, second = jax.random.split(key)
    base = jax.random.randint(first, (2, NT, NT), 0, SLOT + 1)
    hottest = jax.random.randint(second, (2, 1, 1), 0, NT)
    dest = lax.broadcasted_iota(jnp.int32, (2, NT, NT), 2)
    return jnp.where(dest == hottest, SLOT, base).astype(jnp.int32)


def place_ends(drawn, stream_key, least, top_value):
    place = [jax.random.randint(jax.random.fold_in(stream_key, axis), (), 0, length) for axis, length in enumerate(drawn.shape)]
    widest = drawn.shape.index(max(drawn.shape))
    beside = place[:widest] + [(place[widest] + 1) % drawn.shape[widest]] + place[widest + 1:]
    return drawn.at[tuple(place)].set(least).at[tuple(beside)].set(top_value)


def levels(own_key, shape, pieces, least, largest):
    def one(position, parts):
        heights = jax.random.uniform(jax.random.fold_in(jax.random.fold_in(own_key, 6), position), (parts,), jnp.float32, least / len(pieces), largest / len(pieces))
        return jnp.repeat(jnp.exp(heights), shape[position] // parts).reshape((-1,) + (1,) * (len(shape) - position - 1))

    factor_of = one(*pieces[0])
    for cut in pieces[1:]:
        factor_of = factor_of * one(*cut)
    return factor_of


def noise(rng, dims, scale, limit, shards=(), held_as=jnp.bfloat16):
    entries = jax.random.normal(rng, dims, jnp.float32) * scale
    if len(shards) > 0:
        entries = levels(rng, dims, shards, -0.22, 0.18) * entries
    return jnp.clip(entries, min=-limit, max=limit).astype(held_as)


def setup_inputs(seed: int = 0) -> dict:
    seeds = jax.random.split(jax.random.key(seed), 11)
    adjoint_state = noise(seeds[0], (2, F, L, NX, NY), 1.0, 6.0, ((0, 2), (3, 32), (4, 4)), jnp.float32)
    land_mask = place_ends((jax.random.randint(seeds[1], (2, NX, NY), 0, 5) < 4).astype(jnp.int32), jax.random.fold_in(seeds[1], 1), 0, 1)
    diffusivity = jnp.clip(jnp.exp(math.log(0.24) - 2.4849066 * jax.random.uniform(seeds[2], (2, NX, NY), jnp.float32) ** levels(seeds[2], (2, NX, NY), ((0, 2), (1, 32), (2, 4)), -0.2, 0.2)), 0.02, 0.24)
    mixing = noise(seeds[3], (2, F, L, L), L ** -0.5, 0.875, ((0, 2),), jnp.float32)
    nudging = jnp.clip(jnp.exp(math.log(1.0) - 2.3025851 * jax.random.uniform(seeds[4], (NX, NY), jnp.float32) ** levels(seeds[4], (NX, NY), ((0, 32), (1, 4)), -0.2, 0.2)), 0.1, 1.0)
    nest_x = place_ends(jax.random.randint(seeds[5], (NT,), 0, CX - CX // 3 + 1), jax.random.fold_in(seeds[5], 1), 0, (CX - CX // 3 + 1) - 1).astype(jnp.int32)
    nest_y = place_ends(jax.random.randint(seeds[6], (NT,), 0, CY - CY // 3 + 1), jax.random.fold_in(seeds[6], 1), 0, (CY - CY // 3 + 1) - 1).astype(jnp.int32)
    obs_forcing = noise(seeds[7], (2, NT, SLOT, NT), 1.0, 6.0, ((0, 2), (1, 128)), jnp.float32)
    obs_cell = place_ends(jax.random.randint(seeds[8], (2, NT, SLOT, NT), 0, F * L * CX * CY), jax.random.fold_in(seeds[8], 1), 0, (F * L * CX * CY) - 1).astype(jnp.int32)
    obs_count = draw_obs_count(jax.random.fold_in(seeds[10], 71), 0)
    return dict(adjoint_state=adjoint_state, land_mask=land_mask, diffusivity=diffusivity, mixing=mixing, nudging=nudging, nest_x=nest_x, nest_y=nest_y, obs_forcing=obs_forcing, obs_cell=obs_cell, obs_count=obs_count)


def spread_field(field, kappa):
    padded = jnp.pad(field, ((0, 0), (0, 0), (1, 1), (1, 1)))
    beside_all = padded[:, :, 2:, 1:-1] + padded[:, :, :-2, 1:-1]
    beside_all = beside_all + padded[:, :, 1:-1, 2:] + padded[:, :, 1:-1, :-2]
    return field + kappa * (beside_all - 4.0 * field)


def grid_step(inputs):
    state, mask_int, kappa, matrix, values, cells, counts, weight = inputs
    mask = mask_int.astype(jnp.float32)
    masked = state * mask[None, None]
    spread = spread_field(masked, kappa)
    flat = spread.reshape(F, L, NX * NY)
    mixed = jnp.einsum("fkl,flc->fkc", matrix.astype(jnp.float32), flat.astype(jnp.float32), precision=lax.Precision.HIGHEST).reshape(F, L, NX, NY)
    tiles_x = NX // CX
    live = jnp.arange(SLOT, dtype=jnp.int32)[None, :, None] < counts[:, None, :]
    dest = jnp.arange(NT, dtype=jnp.int32)[None, None, :]
    tile_y = dest // tiles_x
    tile_x = dest % tiles_x
    field_idx = cells // (L * CX * CY)
    level_idx = (cells // (CX * CY)) % L
    x_idx = tile_x * CX + (cells // CY) % CX
    y_idx = tile_y * CY + cells % CY
    forced = mixed.at[field_idx, level_idx, x_idx, y_idx].add(jnp.where(live, values, jnp.zeros_like(values)))
    reduced = (weight * mixed).reshape(F, L, tiles_x, CX // 3, 3, NY // CY, CY // 3, 3).sum(axis=(4, 7))
    return forced, reduced, mixed


def reference(adjoint_state, land_mask, diffusivity, mixing, nudging, nest_x, nest_y, obs_forcing, obs_cell, obs_count):
    weights = jnp.stack([nudging, nudging])
    forced, reduced, mixed = lax.map(grid_step, (adjoint_state, land_mask, diffusivity, mixing, obs_forcing, obs_cell, obs_count, weights))
    tiles_x = NX // CX
    tiles_y = NY // CY
    off_x = nest_x.reshape(tiles_y, tiles_x)
    off_y = nest_y.reshape(tiles_y, tiles_x)
    tx_grid = jnp.arange(tiles_x, dtype=jnp.int32)[None, :]
    ty_grid = jnp.arange(tiles_y, dtype=jnp.int32)[:, None]
    x_rows = (tx_grid * CX + off_x)[:, :, None] + jnp.arange(CX // 3, dtype=jnp.int32)[None, None, :]
    y_rows = (ty_grid * CY + off_y)[:, :, None] + jnp.arange(CY // 3, dtype=jnp.int32)[None, None, :]
    xi = x_rows[:, :, :, None]
    yi = y_rows[:, :, None, :]
    block = mixed[1][:, :, xi, yi]
    child_red = jnp.transpose(reduced[0], (0, 1, 4, 2, 3, 5))
    parent = forced[1].at[:, :, xi, yi].add(child_red - block)
    block_t = jnp.transpose(block, (0, 1, 3, 4, 2, 5))
    spread_back = jnp.repeat(jnp.repeat(block_t, 3, axis=3), 3, axis=5).reshape(F, L, NX, NY) / 9.0
    child = forced[0] + spread_back
    masks = land_mask.astype(jnp.float32)
    return jnp.stack([child * masks[0][None, None], parent * masks[1][None, None]])
```

```python
import functools

import jax
import jax.numpy as jnp
from jax import lax
from jax.experimental import pallas as pl
from jax.experimental.pallas import tpu as pltpu
from jax.sharding import PartitionSpec as P

MESH = pl.DeviceIdType.MESH
F32 = jnp.float32
BF16 = jnp.bfloat16
NF, NL, NXC, NYC = 5, 50, 12, 384
LP = 56
NB = NYC // 128
ROWS = NL * NXC * NB
STEP = NXC * NB
NTY, NTX, NYA, NZA = 4, 32, 4, 8
SLOTS = 16


def split(value):
    high = value.astype(BF16)
    low = (value - high.astype(F32)).astype(BF16)
    return high, low


def exchange_kernel(
    nest_x, nest_y, state, mask, kappa, nudge, mix, obs,
    out, obs_out,
    raw, ms, xs, mc, mx, wsel, wback, lhs, pay, got, dlt, cu,
    ycols, yhalo, oa, ob, oc, od, oe, og,
    in_sem, hs_sem, hr_sem, ys_sem, yr_sem, gs_sem, gr_sem,
    os1, or1, os2, or2, os3, or3,
):
    grp = lax.axis_index("grp")
    ty = lax.axis_index("ty")
    tx = lax.axis_index("tx")
    ya, za = tx // NZA, tx % NZA
    child = grp == 0
    parent = grp == 1

    def dev(g=None, y=None, x=None):
        return (grp if g is None else g, ty if y is None else y, tx if x is None else x)

    def fetch(f):
        return pltpu.make_async_copy(state.at[f], raw.at[f], in_sem.at[f])

    for f in range(NF):
        fetch(f).start()

    barrier = pltpu.get_barrier_semaphore()

    def greet(target):
        pl.semaphore_signal(barrier, inc=1, device_id=target, device_id_type=MESH)

    has_left, has_right = tx > 0, tx < NTX - 1
    has_down, has_up = ty > 0, ty < NTY - 1
    greet(dev(g=1 - grp))
    for d in range(1, NTY):
        greet(dev(y=(ty + d) % NTY))
    for d in range(1, NYA):
        greet(dev(x=((ya + d) % NYA) * NZA + za))
    for d in range(1, NZA):
        greet(dev(x=ya * NZA + (za + d) % NZA))

    @pl.when(has_left)
    def _():
        greet(dev(x=tx - 1))

    @pl.when(has_right)
    def _():
        greet(dev(x=tx + 1))

    oa[:, 0:SLOTS] = obs[...].T
    lane = lax.broadcasted_iota(jnp.int32, (NL, 128), 1)
    scale = jnp.where(child, 3, 1)
    off = jnp.where(child, 0, nest_y[0])

    def selection(shape, ydim):
        d = lax.broadcasted_iota(jnp.int32, shape, ydim)
        d = d - scale * lax.broadcasted_iota(jnp.int32, shape, 1 - ydim) - off
        return jnp.where((d >= 0) & (d < scale), 1.0, 0.0).astype(BF16)

    wsel[...] = selection((NYC, 128), 0)
    wback[...] = selection((128, NYC), 1)
    mc[...] = jnp.zeros_like(mc)
    xs[...] = jnp.zeros_like(xs)
    for f in range(NF):
        high, low = split(mix[f])
        mc[f, 0:NL, 0:NL] = high
        mc[f, 0:NL, 64:64 + NL] = high
        mc[f, 0:NL, 128:128 + NL] = low
    cu[4] = jnp.zeros(cu.shape[1:], F32)
    ycols[...] = jnp.zeros_like(ycols)

    @pl.when(tx == 0)
    def _():
        for f in range(NF):
            ms[f, 0] = jnp.zeros(ms.shape[2:], F32)

    @pl.when(tx == NTX - 1)
    def _():
        for f in range(NF):
            ms[f, NXC + 1] = jnp.zeros(ms.shape[2:], F32)

    @pl.when(ty == 0)
    def _():
        yhalo[0] = jnp.zeros(yhalo.shape[1:], F32)

    @pl.when(ty == NTY - 1)
    def _():
        yhalo[1] = jnp.zeros(yhalo.shape[1:], F32)

    pl.semaphore_wait(
        barrier,
        1 + (NTY - 1) + (NYA - 1) + (NZA - 1) + jnp.where(has_left, 1, 0) + jnp.where(has_right, 1, 0),
    )

    def obs1(d):
        peer = (ty + d) % NTY
        return pltpu.make_async_remote_copy(
            oa.at[pl.ds(pl.multiple_of(peer * NTX, NTX), NTX)], ob.at[ty], os1.at[d - 1], or1.at[d - 1],
            device_id=dev(y=peer), device_id_type=MESH,
        )

    def obs2(d):
        peer = (ya + d) % NYA
        return pltpu.make_async_remote_copy(
            oc.at[pl.ds(pl.multiple_of(peer * NZA, NZA), NZA)],
            od.at[pl.ds(pl.multiple_of(ya * NZA, NZA), NZA)], os2.at[d - 1], or2.at[d - 1],
            device_id=dev(x=peer * NZA + za), device_id_type=MESH,
        )

    def obs3(d):
        peer = (za + d) % NZA
        return pltpu.make_async_remote_copy(
            oe.at[peer], og.at[za], os3.at[d - 1], or3.at[d - 1],
            device_id=dev(x=ya * NZA + peer), device_id_type=MESH,
        )

    for d in range(1, NTY):
        obs1(d).start()

    def halo(f, side):
        source, target, x = (1, NXC + 1, tx - 1) if side == 0 else (NXC, 0, tx + 1)
        return pltpu.make_async_remote_copy(
            ms.at[f, source], ms.at[f, target], hs_sem.at[side, f], hr_sem.at[side, f],
            device_id=dev(x=x), device_id_type=MESH,
        )

    def plane(f, x):
        for b in range(NB):
            r = x * NB + b
            ms[f, x + 1, b, 0:NL] = raw[f, pl.ds(r, NL, stride=STEP), :] * mask[r].astype(F32)

    def edges(f, carry):
        fetch(f).wait()
        plane(f, 0)
        plane(f, NXC - 1)

        @pl.when(has_left)
        def _():
            halo(f, 0).start()

        @pl.when(has_right)
        def _():
            halo(f, 1).start()

        return carry

    lax.fori_loop(0, NF, edges, 0)

    def planes(f, carry):
        first, last = carry
        for x in range(1, NXC - 1):
            plane(f, x)
        for x in range(NXC):
            here = lane == f * NXC + x
            first = jnp.where(here, ms[f, x + 1, 0, 0:NL, 0:1], first)
            last = jnp.where(here, ms[f, x + 1, NB - 1, 0:NL, 127:128], last)
        return first, last

    zero = jnp.zeros((NL, 128), F32)
    first, last = lax.fori_loop(0, NF, planes, (zero, zero))
    ycols[0, 0:NL] = first
    ycols[1, 0:NL] = last

    def yedge(side):
        return pltpu.make_async_remote_copy(
            ycols.at[side], yhalo.at[1 - side], ys_sem.at[side], yr_sem.at[side],
            device_id=dev(y=ty - 1 if side == 0 else ty + 1), device_id_type=MESH,
        )

    @pl.when(has_down)
    def _():
        yedge(0).start()

    @pl.when(has_up)
    def _():
        yedge(1).start()

    for d in range(1, NTY):
        obs1(d).wait_recv()
    ob[ty] = oa[pl.ds(pl.multiple_of(ty * NTX, NTX), NTX), :]
    for s in range(NTY):
        oc[:, s * SLOTS:(s + 1) * SLOTS] = ob[s, :, 0:SLOTS]
    for d in range(1, NYA):
        obs2(d).start()

    @pl.when(has_down)
    def _():
        yedge(1).wait_recv()

    @pl.when(has_up)
    def _():
        yedge(0).wait_recv()

    def feedback(f):
        return pltpu.make_async_remote_copy(
            pay.at[f], got.at[f], gs_sem.at[f], gr_sem.at[f],
            device_id=dev(g=1 - grp), device_id_type=MESH,
        )

    def keep(ref, i, value):
        high, low = split(value)
        ref[i * 64:i * 64 + NL] = high
        ref[256 + i * 64:256 + i * 64 + NL] = low

    def both(result, i):
        return result[i * 64:i * 64 + NL] + result[256 + i * 64:256 + i * 64 + NL]

    def advance(f, carry):
        @pl.when(has_left)
        def _():
            halo(f, 1).wait_recv()

        @pl.when(has_right)
        def _():
            halo(f, 0).wait_recv()

        turn = lax.rem(128 - f * NXC, 128)
        below = pltpu.roll(yhalo[0, 0:LP], turn, axis=1)
        above = pltpu.roll(yhalo[1, 0:LP], turn, axis=1)
        lanes = lax.broadcasted_iota(jnp.int32, (LP, 128), 1)
        for pair in range(NXC // 2):
            for half in range(2):
                x = 2 * pair + half
                cells = [ms[f, x + 1, b] for b in range(NB)]
                up = [pltpu.roll(c, 1, axis=1) for c in cells]
                down = [pltpu.roll(c, 127, axis=1) for c in cells]
                edge_low = below if x == 0 else pltpu.roll(below, 128 - x, axis=1)
                edge_high = pltpu.roll(above, 127 - x, axis=1)
                for b in range(NB):
                    prev = jnp.where(lanes == 0, up[b - 1] if b else edge_low, up[b])
                    after = jnp.where(lanes == 127, down[b + 1] if b < NB - 1 else edge_high, down[b])
                    beside = ms[f, x, b] + ms[f, x + 2, b] + prev + after
                    spread = cells[b] + kappa[x * NB + b] * (beside - 4.0 * cells[b])
                    high, low = split(spread[0:NL])
                    col = half * NYC + b * 128
                    xs[pair, 0:NL, col:col + 128] = high
                    xs[pair, 64:64 + NL, col:col + 128] = low
                    xs[pair, 128:128 + NL, col:col + 128] = high
            mixed = jnp.dot(mc[f], xs[pair], preferred_element_type=F32)
            mx[f, 2 * pair] = mixed[0:LP, 0:NYC]
            mx[f, 2 * pair + 1] = mixed[0:LP, NYC:]

        @pl.when(child)
        def _():
            for i in range(4):
                total = mx[f, 3 * i, 0:NL] * nudge[3 * i:3 * i + 1, :]
                for a in range(1, 3):
                    total = total + mx[f, 3 * i + a, 0:NL] * nudge[3 * i + a:3 * i + a + 1, :]
                keep(lhs, i, total)

        @pl.when(parent)
        def _():
            for i in range(4):
                keep(lhs, i, mx[f, nest_x[0] + i, 0:NL])

        picked = jnp.dot(lhs[...], wsel[...], preferred_element_type=F32)
        for i in range(4):
            pay[f, i, 0:NL] = both(picked, i)
        feedback(f).start()

        @pl.when(f == 1)
        def _():
            for d in range(1, NYA):
                obs2(d).wait_recv()
            own = pl.ds(pl.multiple_of(ya * NZA, NZA), NZA)
            od[own, :] = oc[own, :]
            for z in range(NZA):
                oe[z, 0:NYA] = od[pl.ds(z, NYA, stride=NZA), :]
            for d in range(1, NZA):
                obs3(d).start()

        return carry

    lax.fori_loop(0, NF, advance, 0)

    take = jnp.where(child, 1.0 / 9.0, 1.0)
    give = jnp.where(child, 0.0, 1.0)

    def finish(f, carry):
        feedback(f).wait_recv()
        for i in range(4):
            keep(dlt, i, got[f, i, 0:NL] * take - pay[f, i, 0:NL] * give)
        laid = jnp.dot(dlt[...], wback[...], preferred_element_type=F32)
        for i in range(4):
            cu[i, 0:NL] = both(laid, i)
        for x in range(NXC):
            p = x - nest_x[0]
            index = jnp.where(child, x // 3, jnp.where((p >= 0) & (p < 4), p, 4))
            done = mx[f, x, 0:NL] + cu[index, 0:NL]
            for b in range(NB):
                out[f, pl.ds(x * NB + b, NL, stride=STEP), :] = done[:, b * 128:(b + 1) * 128]
        return carry

    lax.fori_loop(0, NF, finish, 0)

    for d in range(1, NZA):
        obs3(d).wait_recv()
    og[za] = oe[za]
    for z in range(NZA):
        obs_out[z * 8:(z + 1) * 8, :] = og[z]

    for d in range(1, NTY):
        obs1(d).wait_send()
    for d in range(1, NYA):
        obs2(d).wait_send()
    for d in range(1, NZA):
        obs3(d).wait_send()

    @pl.when(has_left)
    def _():
        for f in range(NF):
            halo(f, 0).wait_send()

    @pl.when(has_right)
    def _():
        for f in range(NF):
            halo(f, 1).wait_send()

    @pl.when(has_down)
    def _():
        yedge(0).wait_send()

    @pl.when(has_up)
    def _():
        yedge(1).wait_send()

    for f in range(NF):
        feedback(f).wait_send()


def scatter_kernel(vals, cells, counts, start, mask, out, base, add0, add1, wide, in_sem, out_sem):
    incoming = pltpu.make_async_copy(start, base, in_sem)
    incoming.start()
    add0[...] = jnp.zeros_like(add0)
    add1[...] = jnp.zeros_like(add1)
    for r in range(2 * STEP):
        wide[r:r + 1, :] = mask[r % STEP].astype(F32)
    lane = lax.broadcasted_iota(jnp.int32, (1, 128), 1)

    def source(i, carry):
        z, y = i // NYA, i % NYA
        for t in range(NTY):
            s = t * NTX + y * NZA + z
            count = counts[0, s]
            for k in range(SLOTS):
                cell = cells[k, s]
                value = jnp.where(k < count, vals[z * 8 + y, t * SLOTS + k], 0.0)
                row = pl.ds(lax.shift_right_logical(cell, 7), 1)
                term = jnp.where(lane == (cell & 127), value, 0.0)
                ref = add1 if k % 2 else add0
                ref[row, :] = ref[row, :] + term
        return carry

    lax.fori_loop(0, NYA * NZA, source, 0)
    incoming.wait()

    def leave(f):
        rows = pl.ds(f * ROWS, ROWS)
        return pltpu.make_async_copy(base.at[rows], out.at[rows], out_sem.at[f])

    for f in range(NF):
        def masked(i, carry):
            rows = pl.ds(pl.multiple_of(f * ROWS + i * 2 * STEP, 8), 2 * STEP)
            base[rows, :] = wide[...] * (base[rows, :] + add0[rows, :] + add1[rows, :])
            return carry

        lax.fori_loop(0, ROWS // (2 * STEP), masked, 0)
        leave(f).start()
    for f in range(NF):
        leave(f).wait()


VM = pl.BlockSpec(memory_space=pltpu.VMEM)
SM = pl.BlockSpec(memory_space=pltpu.SMEM)
ANY = pl.BlockSpec(memory_space=pl.ANY)
DMA = pltpu.SemaphoreType.DMA


def local(
    adjoint_state, land_mask, diffusivity, mixing, nudging, nest_x, nest_y, obs_forcing, obs_cell, obs_count
):
    state = adjoint_state.reshape(NF, ROWS, 128)
    mask = land_mask.reshape(STEP, 1, 128)
    kappa = diffusivity.reshape(STEP, 1, 128)
    cells = jnp.transpose(obs_cell[0, :, :, 0])
    counts = obs_count[0, :, 0].reshape(1, -1)
    scratch = [
        pltpu.VMEM((NF, ROWS, 128), F32),
        pltpu.VMEM((NF, NXC + 2, NB, LP, 128), F32),
        pltpu.VMEM((NXC // 2, 192, 2 * NYC), BF16),
        pltpu.VMEM((NF, 64, 192), BF16),
        pltpu.VMEM((NF, NXC, LP, NYC), F32),
        pltpu.VMEM((NYC, 128), BF16),
        pltpu.VMEM((128, NYC), BF16),
        pltpu.VMEM((512, NYC), BF16),
        pltpu.VMEM((NF, 4, LP, 128), F32),
        pltpu.VMEM((NF, 4, LP, 128), F32),
        pltpu.VMEM((512, 128), BF16),
        pltpu.VMEM((5, LP, NYC), F32),
        pltpu.VMEM((2, LP, 128), F32),
        pltpu.VMEM((2, LP, 128), F32),
        pltpu.VMEM((128, 128), F32),
        pltpu.VMEM((NTY, NTX, 128), F32),
        pltpu.VMEM((NTX, 128), F32),
        pltpu.VMEM((NTX, 128), F32),
        pltpu.VMEM((NZA, 8, 128), F32),
        pltpu.VMEM((NZA, 8, 128), F32),
        DMA((NF,)), DMA((2, NF)), DMA((2, NF)), DMA((2,)), DMA((2,)), DMA((NF,)), DMA((NF,)),
        DMA((NTY - 1,)), DMA((NTY - 1,)), DMA((NYA - 1,)), DMA((NYA - 1,)), DMA((NZA - 1,)), DMA((NZA - 1,)),
    ]
    partial, arrived = pl.pallas_call(
        exchange_kernel,
        out_shape=(
            jax.ShapeDtypeStruct((NF, ROWS, 128), F32),
            jax.ShapeDtypeStruct((NZA * 8, 128), F32),
        ),
        in_specs=[SM, SM, ANY, VM, VM, VM, VM, VM],
        out_specs=(VM, VM),
        scratch_shapes=scratch,
        compiler_params=pltpu.CompilerParams(
            collective_id=0, has_side_effects=True, vmem_limit_bytes=44 * 2**20
        ),
        name="exchange",
    )(nest_x, nest_y, state, mask, kappa, nudging, mixing[0], obs_forcing[0, 0])
    total = NF * ROWS
    result = pl.pallas_call(
        scatter_kernel,
        out_shape=jax.ShapeDtypeStruct((total, 128), F32),
        in_specs=[SM, SM, SM, ANY, VM],
        out_specs=ANY,
        scratch_shapes=[
            pltpu.VMEM((total, 128), F32), pltpu.VMEM((total, 128), F32), pltpu.VMEM((total, 128), F32),
            pltpu.VMEM((2 * STEP, 128), F32), DMA, DMA((NF,)),
        ],
        compiler_params=pltpu.CompilerParams(vmem_limit_bytes=24 * 2**20),
        name="scatter",
    )(arrived, cells, counts, partial.reshape(total, 128), mask)
    return result.reshape(1, NF, NL, NXC, NYC)


def solution(mesh):
    in_specs = (
        P("grp", None, None, "tx", "ty"),
        P("grp", "tx", "ty"),
        P("grp", "tx", "ty"),
        P("grp", None, None, None),
        P("tx", "ty"),
        P(("ty", "tx")),
        P(("ty", "tx")),
        P("grp", ("ty", "tx"), None, None),
        P("grp", None, None, ("ty", "tx")),
        P("grp", None, ("ty", "tx")),
    )
    out_specs = P("grp", None, None, "tx", "ty")
    return jax.shard_map(local, mesh=mesh, in_specs=in_specs, out_specs=out_specs, check_vma=False)
```

```python
import functools

import jax
import jax.numpy as jnp
from jax import lax
from jax.experimental import pallas as pl
from jax.experimental.pallas import tpu as pltpu
from jax.sharding import PartitionSpec as P

MESH = pl.DeviceIdType.MESH
F32 = jnp.float32
BF16 = jnp.bfloat16
NF, NL, NXC, NYC = 5, 50, 12, 384
LP = 56
NB = NYC // 128
ROWS = NL * NXC * NB
STEP = NXC * NB
NTY, NTX, NYA, NZA = 4, 32, 4, 8
SLOTS = 16
AHEAD = 2
VMEM_BYTES = 63 * 2**20


def split(value):
    high = value.astype(BF16)
    low = (value - high.astype(F32)).astype(BF16)
    return high, low


def exchange_kernel(
    nest_x_in, nest_y_in, state, mask_in, kappa_in, nudge_in, mix_in, obs_in,
    out, obs_out,
    nest_x, nest_y, mask, kappa, nudge, mix, obs, packed,
    raw, ms, xs, mc, mx, wsel, wback, lhs, pay, got, dlt, cu,
    ycols, yhalo, oa, ob, oc, od, oe, og,
    in_sem, hs_sem, hr_sem, ys_sem, yr_sem, gs_sem, gr_sem,
    os1, or1, os2, or2, os3, or3, small_sem, far_sem, out_sem,
):
    grp = lax.axis_index("grp")
    ty = lax.axis_index("ty")
    tx = lax.axis_index("tx")
    ya, za = tx // NZA, tx % NZA
    child = grp == 0
    parent = grp == 1

    def dev(g=None, y=None, x=None):
        return (grp if g is None else g, ty if y is None else y, tx if x is None else x)

    def fetch(f):
        return pltpu.make_async_copy(state.at[f], raw.at[f], in_sem.at[f])

    smalls = [
        pltpu.make_async_copy(source, target, small_sem.at[i])
        for i, (source, target) in enumerate(
            [(obs_in, obs), (mask_in, mask), (mix_in, mix), (nest_x_in, nest_x), (nest_y_in, nest_y),
             (kappa_in, kappa), (nudge_in, nudge)]
        )
    ]
    smalls[0].start()
    smalls[1].start()
    for f in range(NF):
        fetch(f).start()
    for copy in smalls[2:]:
        copy.start()

    barrier = pltpu.get_barrier_semaphore()

    def greet(target):
        pl.semaphore_signal(barrier, inc=1, device_id=target, device_id_type=MESH)

    has_left, has_right = tx > 0, tx < NTX - 1
    has_down, has_up = ty > 0, ty < NTY - 1
    ring = (
        dev(y=(ty + 1) % NTY), dev(y=(ty + 3) % NTY),
        dev(x=((ya + 1) % NYA) * NZA + za), dev(x=((ya + 3) % NYA) * NZA + za),
        dev(x=ya * NZA + (za + 1) % NZA), dev(x=ya * NZA + (za + 7) % NZA),
    )
    greet(dev(g=1 - grp))
    for device in ring:
        greet(device)
    wrap_left = (za == 0) & has_left
    wrap_right = (za == NZA - 1) & has_right

    @pl.when(wrap_left)
    def _():
        greet(dev(x=tx - 1))

    @pl.when(wrap_right)
    def _():
        greet(dev(x=tx + 1))

    def vouch(stage, sides):
        for side in sides:
            pl.semaphore_signal(
                far_sem.at[stage, side], inc=1, device_id=ring[side], device_id_type=MESH
            )

    def vouched(stage, sides):
        for side in sides:
            pl.semaphore_wait(far_sem.at[stage, side], 1)

    for copy in smalls:
        copy.wait()
    oa[:, 0:SLOTS] = obs[...].T
    lane = lax.broadcasted_iota(jnp.int32, (NL, 128), 1)
    scale = jnp.where(child, 3, 1)
    off = jnp.where(child, 0, nest_y[0])

    def selection(shape, ydim):
        d = lax.broadcasted_iota(jnp.int32, shape, ydim)
        d = d - scale * lax.broadcasted_iota(jnp.int32, shape, 1 - ydim) - off
        return jnp.where((d >= 0) & (d < scale), 1.0, 0.0).astype(BF16)

    wsel[...] = selection((NYC, 128), 0)
    wback[...] = selection((128, NYC), 1)
    mc[...] = jnp.zeros_like(mc)
    xs[...] = jnp.zeros_like(xs)
    for f in range(NF):
        high, low = split(mix[f, :, 0, :])
        mc[f, 0:NL, 0:NL] = high
        mc[f, 0:NL, 64:64 + NL] = high
        mc[f, 0:NL, 128:128 + NL] = low
    cu[4] = jnp.zeros(cu.shape[1:], F32)
    ycols[...] = jnp.zeros_like(ycols)

    @pl.when(tx == 0)
    def _():
        for f in range(NF):
            ms[f, 0] = jnp.zeros(ms.shape[2:], F32)

    @pl.when(tx == NTX - 1)
    def _():
        for f in range(NF):
            ms[f, NXC + 1] = jnp.zeros(ms.shape[2:], F32)

    @pl.when(ty == 0)
    def _():
        yhalo[0] = jnp.zeros(yhalo.shape[1:], F32)

    @pl.when(ty == NTY - 1)
    def _():
        yhalo[1] = jnp.zeros(yhalo.shape[1:], F32)

    pl.semaphore_wait(barrier, 1 + len(ring) + jnp.where(wrap_left | wrap_right, 1, 0))
    vouch(0, range(6))

    def obs1(d):
        peer = (ty + d) % NTY
        return pltpu.make_async_remote_copy(
            oa.at[pl.ds(pl.multiple_of(peer * NTX, NTX), NTX)], ob.at[ty], os1.at[d - 1], or1.at[d - 1],
            device_id=dev(y=peer), device_id_type=MESH,
        )

    def obs2(d):
        peer = (ya + d) % NYA
        return pltpu.make_async_remote_copy(
            oc.at[pl.ds(pl.multiple_of(peer * NZA, NZA), NZA)],
            od.at[pl.ds(pl.multiple_of(ya * NZA, NZA), NZA)], os2.at[d - 1], or2.at[d - 1],
            device_id=dev(x=peer * NZA + za), device_id_type=MESH,
        )

    def obs3(d):
        peer = (za + d) % NZA
        return pltpu.make_async_remote_copy(
            oe.at[peer], og.at[za], os3.at[d - 1], or3.at[d - 1],
            device_id=dev(x=ya * NZA + peer), device_id_type=MESH,
        )

    def halo(f, side):
        source, target, x = (1, NXC + 1, tx - 1) if side == 0 else (NXC, 0, tx + 1)
        return pltpu.make_async_remote_copy(
            ms.at[f, source, :, pl.ds(0, NL)], ms.at[f, target, :, pl.ds(0, NL)], hs_sem.at[side, f], hr_sem.at[side, f],
            device_id=dev(x=x), device_id_type=MESH,
        )

    def send_halo(f):
        @pl.when(has_left)
        def _():
            halo(f, 0).start()

        @pl.when(has_right)
        def _():
            halo(f, 1).start()

    def plane(f, x):
        for b in range(NB):
            r = x * NB + b
            ms[f, x + 1, b, 0:NL] = raw[f, pl.ds(r, NL, stride=STEP), :] * mask[r].astype(F32)

    def edges(f, carry):
        fetch(f).wait()
        plane(f, 0)
        plane(f, NXC - 1)

        @pl.when(f < AHEAD)
        def _():
            send_halo(f)

        return carry

    lax.fori_loop(0, NF, edges, 0)

    def planes(f, carry):
        first, last = carry
        for x in range(1, NXC - 1):
            plane(f, x)
        for x in range(NXC):
            here = lane == f * NXC + x
            first = jnp.where(here, ms[f, x + 1, 0, 0:NL, 0:1], first)
            last = jnp.where(here, ms[f, x + 1, NB - 1, 0:NL, 127:128], last)
        return first, last

    zero = jnp.zeros((NL, 128), F32)
    first, last = lax.fori_loop(0, NF, planes, (zero, zero))
    ycols[0, 0:NL] = first
    ycols[1, 0:NL] = last

    def yedge(side):
        return pltpu.make_async_remote_copy(
            ycols.at[side, pl.ds(0, NL)], yhalo.at[1 - side, pl.ds(0, NL)], ys_sem.at[side], yr_sem.at[side],
            device_id=dev(y=ty - 1 if side == 0 else ty + 1), device_id_type=MESH,
        )

    @pl.when(has_down)
    def _():
        yedge(0).start()

    @pl.when(has_up)
    def _():
        yedge(1).start()

    vouched(0, range(6))
    vouch(1, (4, 5))
    for d in range(1, NTY):
        obs1(d).start()

    @pl.when(has_down)
    def _():
        yedge(1).wait_recv()

    @pl.when(has_up)
    def _():
        yedge(0).wait_recv()

    def feedback(f):
        return pltpu.make_async_remote_copy(
            pay.at[f, :, pl.ds(0, NL)], got.at[f, :, pl.ds(0, NL)], gs_sem.at[f], gr_sem.at[f],
            device_id=dev(g=1 - grp), device_id_type=MESH,
        )

    def keep(ref, i, value):
        high, low = split(value)
        ref[i * 64:i * 64 + NL] = high
        ref[256 + i * 64:256 + i * 64 + NL] = low

    def both(result, i):
        return result[i * 64:i * 64 + NL] + result[256 + i * 64:256 + i * 64 + NL]

    def advance(f, carry):
        @pl.when(f + AHEAD < NF)
        def _():
            send_halo(f + AHEAD)

        @pl.when(has_left)
        def _():
            halo(f, 1).wait_recv()

        @pl.when(has_right)
        def _():
            halo(f, 0).wait_recv()

        turn = lax.rem(128 - f * NXC, 128)
        below = pltpu.roll(yhalo[0, 0:LP], turn, axis=1)
        above = pltpu.roll(yhalo[1, 0:LP], turn, axis=1)
        lanes = lax.broadcasted_iota(jnp.int32, (LP, 128), 1)
        for pair in range(NXC // 2):
            for half in range(2):
                x = 2 * pair + half
                cells = [ms[f, x + 1, b] for b in range(NB)]
                up = [pltpu.roll(c, 1, axis=1) for c in cells]
                down = [pltpu.roll(c, 127, axis=1) for c in cells]
                edge_low = below if x == 0 else pltpu.roll(below, 128 - x, axis=1)
                edge_high = pltpu.roll(above, 127 - x, axis=1)
                for b in range(NB):
                    prev = jnp.where(lanes == 0, up[b - 1] if b else edge_low, up[b])
                    after = jnp.where(lanes == 127, down[b + 1] if b < NB - 1 else edge_high, down[b])
                    beside = ms[f, x, b] + ms[f, x + 2, b] + prev + after
                    spread = cells[b] + kappa[x * NB + b] * (beside - 4.0 * cells[b])
                    high, low = split(spread[0:NL])
                    col = half * NYC + b * 128
                    xs[pair, 0:NL, col:col + 128] = high
                    xs[pair, 64:64 + NL, col:col + 128] = low
                    xs[pair, 128:128 + NL, col:col + 128] = high
            mixed = jnp.dot(mc[f], xs[pair], preferred_element_type=F32)
            mx[f, 2 * pair] = mixed[0:LP, 0:NYC]
            mx[f, 2 * pair + 1] = mixed[0:LP, NYC:]

        @pl.when(child)
        def _():
            for i in range(4):
                total = mx[f, 3 * i, 0:NL] * nudge[3 * i:3 * i + 1, :]
                for a in range(1, 3):
                    total = total + mx[f, 3 * i + a, 0:NL] * nudge[3 * i + a:3 * i + a + 1, :]
                keep(lhs, i, total)

        @pl.when(parent)
        def _():
            for i in range(4):
                keep(lhs, i, mx[f, nest_x[0] + i, 0:NL])

        picked = jnp.dot(lhs[...], wsel[...], preferred_element_type=F32)
        for i in range(4):
            pay[f, i, 0:NL] = both(picked, i)
        feedback(f).start()

        @pl.when(f == 0)
        def _():
            vouched(1, (4, 5))
            vouch(2, (4, 5))
            for d in range(1, NTY):
                obs1(d).wait_recv()
            ob[ty] = oa[pl.ds(pl.multiple_of(ty * NTX, NTX), NTX), :]
            for s in range(NTY):
                oc[:, s * SLOTS:(s + 1) * SLOTS] = ob[s, :, 0:SLOTS]
            for d in range(1, NYA):
                obs2(d).start()

        @pl.when(f == 2)
        def _():
            vouched(2, (4, 5))
            for d in range(1, NYA):
                obs2(d).wait_recv()
            own = pl.ds(pl.multiple_of(ya * NZA, NZA), NZA)
            od[own, :] = oc[own, :]
            for z in range(NZA):
                oe[z, 0:NYA] = od[pl.ds(z, NYA, stride=NZA), :]
            for d in range(1, NZA):
                obs3(d).start()

        return carry

    lax.fori_loop(0, NF, advance, 0)

    take = jnp.where(child, 1.0 / 9.0, 1.0)
    give = jnp.where(child, 0.0, 1.0)

    def finish(f, carry):
        feedback(f).wait_recv()
        for i in range(4):
            keep(dlt, i, got[f, i, 0:NL] * take - pay[f, i, 0:NL] * give)
        laid = jnp.dot(dlt[...], wback[...], preferred_element_type=F32)
        for i in range(4):
            cu[i, 0:NL] = both(laid, i)
        for x in range(NXC):
            p = x - nest_x[0]
            index = jnp.where(child, x // 3, jnp.where((p >= 0) & (p < 4), p, 4))
            done = mx[f, x, 0:NL] + cu[index, 0:NL]
            for b in range(NB):
                raw[f, pl.ds(x * NB + b, NL, stride=STEP), :] = done[:, b * 128:(b + 1) * 128]
        leave(f).start()
        return carry

    def leave(f):
        return pltpu.make_async_copy(raw.at[f], out.at[f], out_sem.at[f])

    lax.fori_loop(0, NF, finish, 0)

    for d in range(1, NZA):
        obs3(d).wait_recv()
    og[za] = oe[za]
    for z in range(NZA):
        packed[z * 8:(z + 1) * 8, :] = og[z]
    leave_obs = pltpu.make_async_copy(packed, obs_out, out_sem.at[NF])
    leave_obs.start()

    for d in range(1, NTY):
        obs1(d).wait_send()
    for d in range(1, NYA):
        obs2(d).wait_send()
    for d in range(1, NZA):
        obs3(d).wait_send()

    @pl.when(has_left)
    def _():
        for f in range(NF):
            halo(f, 0).wait_send()

    @pl.when(has_right)
    def _():
        for f in range(NF):
            halo(f, 1).wait_send()

    @pl.when(has_down)
    def _():
        yedge(0).wait_send()

    @pl.when(has_up)
    def _():
        yedge(1).wait_send()

    for f in range(NF):
        feedback(f).wait_send()
        leave(f).wait()
    leave_obs.wait()


def scatter_kernel(
    vals_in, cells_in, counts_in, start_in, mask_in,
    out, vals, cells, counts, start, mask, terms, wide, index, add0, add1, in_sem, out_sem,
):
    fetches = [
        pltpu.make_async_copy(source, target, in_sem.at[i])
        for i, (source, target) in enumerate(
            [(vals_in, vals), (cells_in, cells), (counts_in, counts), (mask_in, mask), (cells_in, index), (start_in, start)]
        )
    ]
    for fetch in fetches:
        fetch.start()
    add0[...] = jnp.zeros_like(add0)
    add1[...] = jnp.zeros_like(add1)
    for fetch in fetches[:5]:
        fetch.wait()
    for r in range(2 * STEP):
        wide[r:r + 1, :] = mask[r % STEP].astype(F32)
    slot = lax.broadcasted_iota(jnp.int32, (SLOTS, 128), 0)
    lane = lax.broadcasted_iota(jnp.int32, (SLOTS, 128), 1)
    lanes = jnp.where(slot < counts[...], cells[...] & 127, -1)
    turned = vals[...].T
    for s in range(NTY * NTX):
        t, y, z = s // NTX, s % NTX // NZA, s % NZA
        value = turned[t * SLOTS:(t + 1) * SLOTS, z * 8 + y:z * 8 + y + 1]
        terms[s * SLOTS:(s + 1) * SLOTS, :] = jnp.where(lane == lanes[:, s:s + 1], value, 0.0)

    def source(i, carry):
        for u in range(4):
            s = i * 4 + u
            for k in range(SLOTS):
                row = pl.ds(lax.shift_right_logical(index[k, s], 7), 1)
                ref = add1 if k % 2 else add0
                ref[row, :] = ref[row, :] + terms[pl.ds(s * SLOTS + k, 1), :]
        return carry

    lax.fori_loop(0, NTY * NTX // 4, source, 0)
    fetches[5].wait()

    def leave(f):
        rows = pl.ds(f * ROWS, ROWS)
        return pltpu.make_async_copy(add0.at[rows], out.at[rows], out_sem.at[f])

    for f in range(NF):
        def masked(i, carry):
            rows = pl.ds(pl.multiple_of(f * ROWS + i * 2 * STEP, 8), 2 * STEP)
            add0[rows, :] = wide[...] * (start[rows, :] + add0[rows, :] + add1[rows, :])
            return carry

        lax.fori_loop(0, ROWS // (2 * STEP), masked, 0)
        leave(f).start()
    for f in range(NF):
        leave(f).wait()


HBM = pl.BlockSpec(memory_space=pltpu.HBM)
DMA = pltpu.SemaphoreType.DMA


def local(
    adjoint_state, land_mask, diffusivity, mixing, nudging, nest_x, nest_y, obs_forcing, obs_cell, obs_count
):
    state = adjoint_state.reshape(NF, ROWS, 128)
    mask = land_mask.reshape(STEP, 1, 128)
    kappa = diffusivity.reshape(STEP, 1, 128)
    cells = jnp.transpose(obs_cell[0, :, :, 0])
    counts = obs_count[0, :, 0].reshape(1, -1)
    scratch = [
        pltpu.SMEM((1,), jnp.int32),
        pltpu.SMEM((1,), jnp.int32),
        pltpu.VMEM((STEP, 1, 128), jnp.int32),
        pltpu.VMEM((STEP, 1, 128), F32),
        pltpu.VMEM((NXC, NYC), F32),
        pltpu.VMEM((NF, NL, 1, NL), F32),
        pltpu.VMEM((SLOTS, 128), F32),
        pltpu.VMEM((NZA * 8, 128), F32),
        pltpu.VMEM((NF, ROWS, 128), F32),
        pltpu.VMEM((NF, NXC + 2, NB, LP, 128), F32),
        pltpu.VMEM((NXC // 2, 192, 2 * NYC), BF16),
        pltpu.VMEM((NF, 64, 192), BF16),
        pltpu.VMEM((NF, NXC, LP, NYC), F32),
        pltpu.VMEM((NYC, 128), BF16),
        pltpu.VMEM((128, NYC), BF16),
        pltpu.VMEM((512, NYC), BF16),
        pltpu.VMEM((NF, 4, LP, 128), F32),
        pltpu.VMEM((NF, 4, LP, 128), F32),
        pltpu.VMEM((512, 128), BF16),
        pltpu.VMEM((5, LP, NYC), F32),
        pltpu.VMEM((2, LP, 128), F32),
        pltpu.VMEM((2, LP, 128), F32),
        pltpu.VMEM((128, 128), F32),
        pltpu.VMEM((NTY, NTX, 128), F32),
        pltpu.VMEM((NTX, 128), F32),
        pltpu.VMEM((NTX, 128), F32),
        pltpu.VMEM((NZA, 8, 128), F32),
        pltpu.VMEM((NZA, 8, 128), F32),
        DMA((NF,)), DMA((2, NF)), DMA((2, NF)), DMA((2,)), DMA((2,)), DMA((NF,)), DMA((NF,)),
        DMA((NTY - 1,)), DMA((NTY - 1,)), DMA((NYA - 1,)), DMA((NYA - 1,)), DMA((NZA - 1,)), DMA((NZA - 1,)),
        DMA((7,)), pltpu.SemaphoreType.REGULAR((3, 6)), DMA((NF + 1,)),
    ]
    partial, arrived = pl.pallas_call(
        exchange_kernel,
        out_shape=(
            jax.ShapeDtypeStruct((NF, ROWS, 128), F32),
            jax.ShapeDtypeStruct((NZA * 8, 128), F32),
        ),
        in_specs=[HBM] * 8,
        out_specs=(HBM, HBM),
        scratch_shapes=scratch,
        compiler_params=pltpu.CompilerParams(
            collective_id=0, has_side_effects=True, vmem_limit_bytes=VMEM_BYTES
        ),
        name="exchange",
    )(nest_x, nest_y, state, mask, kappa, nudging, mixing.reshape(NF, NL, 1, NL), obs_forcing[0, 0])
    total = NF * ROWS
    result = pl.pallas_call(
        scatter_kernel,
        out_shape=jax.ShapeDtypeStruct((total, 128), F32),
        in_specs=[HBM] * 5,
        out_specs=HBM,
        scratch_shapes=[
            pltpu.VMEM((NZA * 8, 128), F32), pltpu.VMEM((SLOTS, NTY * NTX), jnp.int32),
            pltpu.VMEM((1, NTY * NTX), jnp.int32), pltpu.VMEM((total, 128), F32), pltpu.VMEM((STEP, 1, 128), jnp.int32),
            pltpu.VMEM((NTY * NTX * SLOTS, 128), F32), pltpu.VMEM((2 * STEP, 128), F32),
            pltpu.SMEM((SLOTS, NTY * NTX), jnp.int32),
            pltpu.VMEM((total, 128), F32), pltpu.VMEM((total, 128), F32), DMA((6,)), DMA((NF,)),
        ],
        compiler_params=pltpu.CompilerParams(vmem_limit_bytes=VMEM_BYTES),
        name="scatter",
    )(arrived, cells, counts, partial.reshape(total, 128), mask)
    return result.reshape(1, NF, NL, NXC, NYC)


def solution(mesh):
    in_specs = (
        P("grp", None, None, "tx", "ty"),
        P("grp", "tx", "ty"),
        P("grp", "tx", "ty"),
        P("grp", None, None, None),
        P("tx", "ty"),
        P(("ty", "tx")),
        P(("ty", "tx")),
        P("grp", ("ty", "tx"), None, None),
        P("grp", None, None, ("ty", "tx")),
        P("grp", None, ("ty", "tx")),
    )
    out_specs = P("grp", None, None, "tx", "ty")
    return jax.shard_map(local, mesh=mesh, in_specs=in_specs, out_specs=out_specs, check_vma=False)
```

```python
import functools

import jax
import jax.numpy as jnp
from jax import lax
from jax.experimental import pallas as pl
from jax.experimental.pallas import tpu as pltpu
from jax.sharding import PartitionSpec as P

MESH = pl.DeviceIdType.MESH
F32 = jnp.float32
BF16 = jnp.bfloat16
NF, NL, NXC, NYC = 5, 50, 12, 384
LP = 56
NB = NYC // 128
ROWS = NL * NXC * NB
STEP = NXC * NB
NTY, NTX, NYA, NZA = 4, 32, 4, 8
SLOTS = 16
AHEAD = 2
VMEM_BYTES = 63 * 2**20


def split(value):
    high = value.astype(BF16)
    low = (value - high.astype(F32)).astype(BF16)
    return high, low


def exchange_kernel(
    nest_x_in, nest_y_in, state, mask_in, kappa_in, nudge_in, mix_in, obs_in,
    out, obs_out,
    nest_x, nest_y, mask, kappa, nudge, mix, obs, packed,
    raw, ms, xs, mc, mx, wsel, wback, lhs, pay, got, dlt, cu,
    ycols, yhalo, oa, ob, oc, od, oe, og,
    in_sem, hs_sem, hr_sem, ys_sem, yr_sem, gs_sem, gr_sem,
    os1, or1, os2, or2, os3, or3, small_sem, far_sem, out_sem,
):
    grp = lax.axis_index("grp")
    ty = lax.axis_index("ty")
    tx = lax.axis_index("tx")
    ya, za = tx // NZA, tx % NZA
    child = grp == 0
    parent = grp == 1

    def dev(g=None, y=None, x=None):
        return (grp if g is None else g, ty if y is None else y, tx if x is None else x)

    def fetch(f):
        return pltpu.make_async_copy(state.at[f], raw.at[f], in_sem.at[f])

    smalls = [
        pltpu.make_async_copy(source, target, small_sem.at[i])
        for i, (source, target) in enumerate(
            [(obs_in, obs), (mask_in, mask), (mix_in, mix), (nest_x_in, nest_x), (nest_y_in, nest_y),
             (kappa_in, kappa), (nudge_in, nudge)]
        )
    ]
    smalls[0].start()
    smalls[1].start()
    for f in range(NF):
        fetch(f).start()
    for copy in smalls[2:]:
        copy.start()

    barrier = pltpu.get_barrier_semaphore()

    def greet(target):
        pl.semaphore_signal(barrier, inc=1, device_id=target, device_id_type=MESH)

    has_left, has_right = tx > 0, tx < NTX - 1
    has_down, has_up = ty > 0, ty < NTY - 1
    ring = (
        dev(y=(ty + 1) % NTY), dev(y=(ty + 3) % NTY),
        dev(x=((ya + 1) % NYA) * NZA + za), dev(x=((ya + 3) % NYA) * NZA + za),
        dev(x=ya * NZA + (za + 1) % NZA), dev(x=ya * NZA + (za + 7) % NZA),
    )
    greet(dev(g=1 - grp))
    for device in ring:
        greet(device)
    wrap_left = (za == 0) & has_left
    wrap_right = (za == NZA - 1) & has_right

    @pl.when(wrap_left)
    def _():
        greet(dev(x=tx - 1))

    @pl.when(wrap_right)
    def _():
        greet(dev(x=tx + 1))

    def vouch(stage, sides):
        for side in sides:
            pl.semaphore_signal(
                far_sem.at[stage, side], inc=1, device_id=ring[side], device_id_type=MESH
            )

    def vouched(stage, sides):
        for side in sides:
            pl.semaphore_wait(far_sem.at[stage, side], 1)

    for copy in smalls:
        copy.wait()
    oa[:, 0:SLOTS] = obs[...].T
    lane = lax.broadcasted_iota(jnp.int32, (NL, 128), 1)
    scale = jnp.where(child, 3, 1)
    off = jnp.where(child, 0, nest_y[0])

    def selection(shape, ydim):
        d = lax.broadcasted_iota(jnp.int32, shape, ydim)
        d = d - scale * lax.broadcasted_iota(jnp.int32, shape, 1 - ydim) - off
        return jnp.where((d >= 0) & (d < scale), 1.0, 0.0).astype(BF16)

    wsel[...] = selection((NYC, 128), 0)
    wback[...] = selection((128, NYC), 1)
    mc[...] = jnp.zeros_like(mc)
    xs[...] = jnp.zeros_like(xs)
    for f in range(NF):
        high, low = split(mix[f, :, 0, :])
        mc[f, 0:NL, 0:NL] = high
        mc[f, 0:NL, 64:64 + NL] = high
        mc[f, 0:NL, 128:128 + NL] = low
    cu[4] = jnp.zeros(cu.shape[1:], F32)

    @pl.when(tx == 0)
    def _():
        for f in range(NF):
            ms[f, 0] = jnp.zeros(ms.shape[2:], F32)

    @pl.when(tx == NTX - 1)
    def _():
        for f in range(NF):
            ms[f, NXC + 1] = jnp.zeros(ms.shape[2:], F32)

    @pl.when(ty == 0)
    def _():
        for part in range(2):
            yhalo[part, 0] = jnp.zeros(yhalo.shape[2:], F32)

    @pl.when(ty == NTY - 1)
    def _():
        for part in range(2):
            yhalo[part, 1] = jnp.zeros(yhalo.shape[2:], F32)

    def obs1(d):
        peer = (ty + d) % NTY
        return pltpu.make_async_remote_copy(
            oa.at[pl.ds(pl.multiple_of(peer * NTX, NTX), NTX)], ob.at[ty], os1.at[d - 1], or1.at[d - 1],
            device_id=dev(y=peer), device_id_type=MESH,
        )

    def obs2(d):
        peer = (ya + d) % NYA
        return pltpu.make_async_remote_copy(
            oc.at[pl.ds(pl.multiple_of(peer * NZA, NZA), NZA)],
            od.at[pl.ds(pl.multiple_of(ya * NZA, NZA), NZA)], os2.at[d - 1], or2.at[d - 1],
            device_id=dev(x=peer * NZA + za), device_id_type=MESH,
        )

    def obs3(d):
        peer = (za + d) % NZA
        return pltpu.make_async_remote_copy(
            oe.at[peer], og.at[za], os3.at[d - 1], or3.at[d - 1],
            device_id=dev(x=ya * NZA + peer), device_id_type=MESH,
        )

    def halo(f, side):
        source, target, x = (1, NXC + 1, tx - 1) if side == 0 else (NXC, 0, tx + 1)
        return pltpu.make_async_remote_copy(
            ms.at[f, source, :, pl.ds(0, NL)], ms.at[f, target, :, pl.ds(0, NL)], hs_sem.at[side, f], hr_sem.at[side, f],
            device_id=dev(x=x), device_id_type=MESH,
        )

    def send_halo(f):
        @pl.when(has_left)
        def _():
            halo(f, 0).start()

        @pl.when(has_right)
        def _():
            halo(f, 1).start()

    def plane(f, x):
        for b in range(NB):
            r = x * NB + b
            ms[f, x + 1, b, 0:NL] = raw[f, pl.ds(r, NL, stride=STEP), :] * mask[r].astype(F32)

    def columns(f, shift, first, last):
        for x in range(NXC):
            here = lane == shift + x
            first = jnp.where(here, ms[f, x + 1, 0, 0:NL, 0:1], first)
            last = jnp.where(here, ms[f, x + 1, NB - 1, 0:NL, 127:128], last)
        return first, last

    def yedge(part, side):
        return pltpu.make_async_remote_copy(
            ycols.at[part, side, pl.ds(0, NL)], yhalo.at[part, 1 - side, pl.ds(0, NL)],
            ys_sem.at[part, side], yr_sem.at[part, side],
            device_id=dev(y=ty - 1 if side == 0 else ty + 1), device_id_type=MESH,
        )

    def send_columns(part, first, last):
        ycols[part, 0, 0:NL] = first
        ycols[part, 1, 0:NL] = last

        @pl.when(has_down)
        def _():
            yedge(part, 0).start()

        @pl.when(has_up)
        def _():
            yedge(part, 1).start()

    def await_columns(part):
        @pl.when(has_down)
        def _():
            yedge(part, 1).wait_recv()

        @pl.when(has_up)
        def _():
            yedge(part, 0).wait_recv()

    zero = jnp.zeros((NL, 128), F32)
    fetch(0).wait()
    for x in (0, NXC - 1, *range(1, NXC - 1)):
        plane(0, x)
    first, last = columns(0, 0, zero, zero)
    pl.semaphore_wait(barrier, 1 + len(ring) + jnp.where(wrap_left | wrap_right, 1, 0))
    send_columns(0, first, last)
    send_halo(0)
    vouch(0, range(6))

    def planes(f, carry):
        first, last = carry
        fetch(f).wait()
        plane(f, 0)
        plane(f, NXC - 1)

        @pl.when(f < AHEAD)
        def _():
            send_halo(f)

        for x in range(1, NXC - 1):
            plane(f, x)
        return columns(f, (f - 1) * NXC, first, last)

    first, last = lax.fori_loop(1, NF, planes, (zero, zero))
    send_columns(1, first, last)

    vouched(0, range(6))
    vouch(1, (4, 5))
    for d in range(1, NTY):
        obs1(d).start()

    def feedback(f, part):
        planes = pl.ds(2 * part, 2)
        return pltpu.make_async_remote_copy(
            pay.at[f, planes, pl.ds(0, NL)], got.at[f, planes, pl.ds(0, NL)],
            gs_sem.at[part, f], gr_sem.at[part, f],
            device_id=dev(g=1 - grp), device_id_type=MESH,
        )

    def keep(ref, i, low_row, value):
        high, low = split(value)
        ref[i * 64:i * 64 + NL] = high
        ref[low_row + i * 64:low_row + i * 64 + NL] = low

    def both(result, i, low_row):
        return result[i * 64:i * 64 + NL] + result[low_row + i * 64:low_row + i * 64 + NL]

    lanes = lax.broadcasted_iota(jnp.int32, (LP, 128), 1)

    def stencil(f, x, pair, half, part, turn):
        below, above = yhalo[part, 0], yhalo[part, 1]
        cells = [ms[f, x + 1, b] for b in range(NB)]
        up = [pltpu.roll(c, 1, axis=1) for c in cells]
        down = [pltpu.roll(c, 127, axis=1) for c in cells]
        edge_low = pltpu.roll(below, lax.rem(turn + 128 - x, 128), axis=1)
        edge_high = pltpu.roll(above, lax.rem(turn + 127 - x, 128), axis=1)
        for b in range(NB):
            prev = jnp.where(lanes == 0, up[b - 1] if b else edge_low, up[b])
            after = jnp.where(lanes == 127, down[b + 1] if b < NB - 1 else edge_high, down[b])
            beside = ms[f, x, b] + ms[f, x + 2, b] + prev + after
            spread = cells[b] + kappa[x * NB + b] * (beside - 4.0 * cells[b])
            high, low = split(spread[0:NL])
            col = half * NYC + b * 128
            xs[pair, 0:NL, col:col + 128] = high
            xs[pair, 64:64 + NL, col:col + 128] = low
            xs[pair, 128:128 + NL, col:col + 128] = high

    def blend(f, pair, x0, x1):
        mixed = jnp.dot(mc[f], xs[pair], preferred_element_type=F32)
        mx[f, x0] = mixed[0:LP, 0:NYC]
        mx[f, x1] = mixed[0:LP, NYC:]

    groups = ((1, 2), (0, 3))

    def give_back(f, part):
        @pl.when(child)
        def _():
            for n, i in enumerate(groups[part]):
                total = mx[f, 3 * i, 0:NL] * nudge[3 * i:3 * i + 1, :]
                for a in range(1, 3):
                    total = total + mx[f, 3 * i + a, 0:NL] * nudge[3 * i + a:3 * i + a + 1, :]
                keep(lhs, n, 128, total)

        @pl.when(parent)
        def _():
            for n, i in enumerate(groups[part]):
                keep(lhs, n, 128, mx[f, nest_x[0] + i, 0:NL])

        picked = jnp.dot(lhs[...], wsel[...], preferred_element_type=F32)
        for n in range(2):
            pay[f, 2 * part + n, 0:NL] = both(picked, n, 128)
        feedback(f, part).start()

    def interior(f, carry):
        @pl.when(f + AHEAD < NF)
        def _():
            send_halo(f + AHEAD)

        @pl.when(f == 0)
        def _():
            await_columns(0)

        @pl.when(f == 1)
        def _():
            await_columns(1)

        part = jnp.minimum(f, 1)
        turn = 128 - (f - part) * NXC
        for pair in range(NXC // 2 - 1):
            stencil(f, 2 * pair + 1, pair, 0, part, turn)
            stencil(f, 2 * pair + 2, pair, 1, part, turn)
            blend(f, pair, 2 * pair + 1, 2 * pair + 2)
        give_back(f, 0)

        @pl.when(f == 0)
        def _():
            vouched(1, (4, 5))
            vouch(2, (4, 5))
            for d in range(1, NTY):
                obs1(d).wait_recv()
            ob[ty] = oa[pl.ds(pl.multiple_of(ty * NTX, NTX), NTX), :]
            for s in range(NTY):
                oc[:, s * SLOTS:(s + 1) * SLOTS] = ob[s, :, 0:SLOTS]
            for d in range(1, NYA):
                obs2(d).start()

        @pl.when(f == 2)
        def _():
            vouched(2, (4, 5))
            for d in range(1, NYA):
                obs2(d).wait_recv()
            own = pl.ds(pl.multiple_of(ya * NZA, NZA), NZA)
            od[own, :] = oc[own, :]
            for z in range(NZA):
                oe[z, 0:NYA] = od[pl.ds(z, NYA, stride=NZA), :]
            for d in range(1, NZA):
                obs3(d).start()

        return carry

    lax.fori_loop(0, NF, interior, 0)

    def border(f, carry):
        @pl.when(has_left)
        def _():
            halo(f, 1).wait_recv()

        @pl.when(has_right)
        def _():
            halo(f, 0).wait_recv()

        part = jnp.minimum(f, 1)
        turn = 128 - (f - part) * NXC
        stencil(f, 0, NXC // 2 - 1, 0, part, turn)
        stencil(f, NXC - 1, NXC // 2 - 1, 1, part, turn)
        blend(f, NXC // 2 - 1, 0, NXC - 1)
        give_back(f, 1)
        return carry

    lax.fori_loop(0, NF, border, 0)

    take = jnp.where(child, 1.0 / 9.0, 1.0)
    give = jnp.where(child, 0.0, 1.0)

    def finish(f, carry):
        for part in range(2):
            feedback(f, part).wait_recv()
        for i in range(4):
            keep(dlt, i, 256, got[f, i, 0:NL] * take - pay[f, i, 0:NL] * give)
        laid = jnp.dot(dlt[...], wback[...], preferred_element_type=F32)
        for n, i in enumerate(groups[0] + groups[1]):
            cu[i, 0:NL] = both(laid, n, 256)
        for x in range(NXC):
            p = x - nest_x[0]
            index = jnp.where(child, x // 3, jnp.where((p >= 0) & (p < 4), p, 4))
            done = mx[f, x, 0:NL] + cu[index, 0:NL]
            for b in range(NB):
                raw[f, pl.ds(x * NB + b, NL, stride=STEP), :] = done[:, b * 128:(b + 1) * 128]
        leave(f).start()
        return carry

    def leave(f):
        return pltpu.make_async_copy(raw.at[f], out.at[f], out_sem.at[f])

    lax.fori_loop(0, NF, finish, 0)

    for d in range(1, NZA):
        obs3(d).wait_recv()
    og[za] = oe[za]
    for z in range(NZA):
        packed[z * 8:(z + 1) * 8, :] = og[z]
    leave_obs = pltpu.make_async_copy(packed, obs_out, out_sem.at[NF])
    leave_obs.start()

    for d in range(1, NTY):
        obs1(d).wait_send()
    for d in range(1, NYA):
        obs2(d).wait_send()
    for d in range(1, NZA):
        obs3(d).wait_send()

    @pl.when(has_left)
    def _():
        for f in range(NF):
            halo(f, 0).wait_send()

    @pl.when(has_right)
    def _():
        for f in range(NF):
            halo(f, 1).wait_send()

    @pl.when(has_down)
    def _():
        for part in range(2):
            yedge(part, 0).wait_send()

    @pl.when(has_up)
    def _():
        for part in range(2):
            yedge(part, 1).wait_send()

    for f in range(NF):
        for part in range(2):
            feedback(f, part).wait_send()
        leave(f).wait()
    leave_obs.wait()


def scatter_kernel(
    vals_in, cells_in, counts_in, start_in, mask_in,
    out, vals, cells, counts, start, mask, terms, wide, index, add0, add1, in_sem, out_sem,
):
    fetches = [
        pltpu.make_async_copy(source, target, in_sem.at[i])
        for i, (source, target) in enumerate(
            [(vals_in, vals), (cells_in, cells), (counts_in, counts), (mask_in, mask), (cells_in, index), (start_in, start)]
        )
    ]
    for fetch in fetches:
        fetch.start()
    add0[...] = jnp.zeros_like(add0)
    add1[...] = jnp.zeros_like(add1)
    for fetch in fetches[:5]:
        fetch.wait()
    for r in range(2 * STEP):
        wide[r:r + 1, :] = mask[r % STEP].astype(F32)
    slot = lax.broadcasted_iota(jnp.int32, (SLOTS, 128), 0)
    lane = lax.broadcasted_iota(jnp.int32, (SLOTS, 128), 1)
    lanes = jnp.where(slot < counts[...], cells[...] & 127, -1)
    turned = vals[...].T
    for s in range(NTY * NTX):
        t, y, z = s // NTX, s % NTX // NZA, s % NZA
        value = turned[t * SLOTS:(t + 1) * SLOTS, z * 8 + y:z * 8 + y + 1]
        terms[s * SLOTS:(s + 1) * SLOTS, :] = jnp.where(lane == lanes[:, s:s + 1], value, 0.0)

    def source(s, carry):
        for k in range(SLOTS):
            row = pl.ds(lax.shift_right_logical(index[k, s], 7), 1)
            ref = add1 if k % 2 else add0
            ref[row, :] = ref[row, :] + terms[pl.ds(s * SLOTS + k, 1), :]
        return carry

    lax.fori_loop(0, NTY * NTX, source, 0)
    fetches[5].wait()

    def leave(f):
        rows = pl.ds(f * ROWS, ROWS)
        return pltpu.make_async_copy(add0.at[rows], out.at[rows], out_sem.at[f])

    for f in range(NF):
        def masked(i, carry):
            rows = pl.ds(pl.multiple_of(f * ROWS + i * 2 * STEP, 8), 2 * STEP)
            add0[rows, :] = wide[...] * (start[rows, :] + add0[rows, :] + add1[rows, :])
            return carry

        lax.fori_loop(0, ROWS // (2 * STEP), masked, 0)
        leave(f).start()
    for f in range(NF):
        leave(f).wait()


HBM = pl.BlockSpec(memory_space=pltpu.HBM)
DMA = pltpu.SemaphoreType.DMA


def local(
    adjoint_state, land_mask, diffusivity, mixing, nudging, nest_x, nest_y, obs_forcing, obs_cell, obs_count
):
    state = adjoint_state.reshape(NF, ROWS, 128)
    mask = land_mask.reshape(STEP, 1, 128)
    kappa = diffusivity.reshape(STEP, 1, 128)
    cells = jnp.transpose(obs_cell[0, :, :, 0])
    counts = obs_count[0, :, 0].reshape(1, -1)
    scratch = [
        pltpu.SMEM((1,), jnp.int32),
        pltpu.SMEM((1,), jnp.int32),
        pltpu.VMEM((STEP, 1, 128), jnp.int32),
        pltpu.VMEM((STEP, 1, 128), F32),
        pltpu.VMEM((NXC, NYC), F32),
        pltpu.VMEM((NF, NL, 1, NL), F32),
        pltpu.VMEM((SLOTS, 128), F32),
        pltpu.VMEM((NZA * 8, 128), F32),
        pltpu.VMEM((NF, ROWS, 128), F32),
        pltpu.VMEM((NF, NXC + 2, NB, LP, 128), F32),
        pltpu.VMEM((NXC // 2, 192, 2 * NYC), BF16),
        pltpu.VMEM((NF, 64, 192), BF16),
        pltpu.VMEM((NF, NXC, LP, NYC), F32),
        pltpu.VMEM((NYC, 128), BF16),
        pltpu.VMEM((128, NYC), BF16),
        pltpu.VMEM((256, NYC), BF16),
        pltpu.VMEM((NF, 4, LP, 128), F32),
        pltpu.VMEM((NF, 4, LP, 128), F32),
        pltpu.VMEM((512, 128), BF16),
        pltpu.VMEM((5, LP, NYC), F32),
        pltpu.VMEM((2, 2, LP, 128), F32),
        pltpu.VMEM((2, 2, LP, 128), F32),
        pltpu.VMEM((128, 128), F32),
        pltpu.VMEM((NTY, NTX, 128), F32),
        pltpu.VMEM((NTX, 128), F32),
        pltpu.VMEM((NTX, 128), F32),
        pltpu.VMEM((NZA, 8, 128), F32),
        pltpu.VMEM((NZA, 8, 128), F32),
        DMA((NF,)), DMA((2, NF)), DMA((2, NF)), DMA((2, 2)), DMA((2, 2)), DMA((2, NF)), DMA((2, NF)),
        DMA((NTY - 1,)), DMA((NTY - 1,)), DMA((NYA - 1,)), DMA((NYA - 1,)), DMA((NZA - 1,)), DMA((NZA - 1,)),
        DMA((7,)), pltpu.SemaphoreType.REGULAR((3, 6)), DMA((NF + 1,)),
    ]
    partial, arrived = pl.pallas_call(
        exchange_kernel,
        out_shape=(
            jax.ShapeDtypeStruct((NF, ROWS, 128), F32),
            jax.ShapeDtypeStruct((NZA * 8, 128), F32),
        ),
        in_specs=[HBM] * 8,
        out_specs=(HBM, HBM),
        scratch_shapes=scratch,
        compiler_params=pltpu.CompilerParams(
            collective_id=0, has_side_effects=True, vmem_limit_bytes=VMEM_BYTES
        ),
        name="exchange",
    )(nest_x, nest_y, state, mask, kappa, nudging, mixing.reshape(NF, NL, 1, NL), obs_forcing[0, 0])
    total = NF * ROWS
    result = pl.pallas_call(
        scatter_kernel,
        out_shape=jax.ShapeDtypeStruct((total, 128), F32),
        in_specs=[HBM] * 5,
        out_specs=HBM,
        scratch_shapes=[
            pltpu.VMEM((NZA * 8, 128), F32), pltpu.VMEM((SLOTS, NTY * NTX), jnp.int32),
            pltpu.VMEM((1, NTY * NTX), jnp.int32), pltpu.VMEM((total, 128), F32), pltpu.VMEM((STEP, 1, 128), jnp.int32),
            pltpu.VMEM((NTY * NTX * SLOTS, 128), F32), pltpu.VMEM((2 * STEP, 128), F32),
            pltpu.SMEM((SLOTS, NTY * NTX), jnp.int32),
            pltpu.VMEM((total, 128), F32), pltpu.VMEM((total, 128), F32), DMA((6,)), DMA((NF,)),
        ],
        compiler_params=pltpu.CompilerParams(vmem_limit_bytes=VMEM_BYTES),
        name="scatter",
    )(arrived, cells, counts, partial.reshape(total, 128), mask)
    return result.reshape(1, NF, NL, NXC, NYC)


def solution(mesh):
    in_specs = (
        P("grp", None, None, "tx", "ty"),
        P("grp", "tx", "ty"),
        P("grp", "tx", "ty"),
        P("grp", None, None, None),
        P("tx", "ty"),
        P(("ty", "tx")),
        P(("ty", "tx")),
        P("grp", ("ty", "tx"), None, None),
        P("grp", None, None, ("ty", "tx")),
        P("grp", None, ("ty", "tx")),
    )
    out_specs = P("grp", None, None, "tx", "ty")
    return jax.shard_map(local, mesh=mesh, in_specs=in_specs, out_specs=out_specs, check_vma=False)
```

```python
import functools

import jax
import jax.numpy as jnp
from jax import lax
from jax.experimental import pallas as pl
from jax.experimental.pallas import tpu as pltpu
from jax.sharding import PartitionSpec as P

MESH = pl.DeviceIdType.MESH
F32 = jnp.float32
BF16 = jnp.bfloat16
NF, NL, NXC, NYC = 5, 50, 12, 384
LP = 56
NB = NYC // 128
ROWS = NL * NXC * NB
STEP = NXC * NB
NTY, NTX, NYA, NZA = 4, 32, 4, 8
SLOTS = 16
AHEAD = 2
VMEM_BYTES = 63 * 2**20


def split(value):
    high = value.astype(BF16)
    low = (value - high.astype(F32)).astype(BF16)
    return high, low


def exchange_kernel(
    nest_x_in, nest_y_in, state, mask_in, kappa_in, nudge_in, mix_in, obs_in,
    out, obs_out,
    nest_x, nest_y, mask, kappa, nudge, mix, obs, packed,
    raw, ms, xs, xe, em, mc, mx, wsel, wback, lhs, pay, got, dlt, cu,
    ycols, yhalo, oa, ob, oc, od, oe, og,
    in_sem, hs_sem, hr_sem, ys_sem, yr_sem, gs_sem, gr_sem,
    os1, or1, os2, or2, os3, or3, small_sem, far_sem, out_sem,
):
    grp = lax.axis_index("grp")
    ty = lax.axis_index("ty")
    tx = lax.axis_index("tx")
    ya, za = tx // NZA, tx % NZA
    child = grp == 0
    parent = grp == 1

    def dev(g=None, y=None, x=None):
        return (grp if g is None else g, ty if y is None else y, tx if x is None else x)

    def fetch(f):
        return pltpu.make_async_copy(state.at[f], raw.at[f], in_sem.at[f])

    smalls = [
        pltpu.make_async_copy(source, target, small_sem.at[i])
        for i, (source, target) in enumerate(
            [(obs_in, obs), (mask_in, mask), (mix_in, mix), (nest_x_in, nest_x), (nest_y_in, nest_y),
             (kappa_in, kappa), (nudge_in, nudge)]
        )
    ]
    smalls[0].start()
    smalls[1].start()
    for f in range(NF):
        fetch(f).start()
    for copy in smalls[2:]:
        copy.start()

    barrier = pltpu.get_barrier_semaphore()

    def greet(target):
        pl.semaphore_signal(barrier, inc=1, device_id=target, device_id_type=MESH)

    has_left, has_right = tx > 0, tx < NTX - 1
    has_down, has_up = ty > 0, ty < NTY - 1
    ring = (
        dev(y=(ty + 1) % NTY), dev(y=(ty + 3) % NTY),
        dev(x=((ya + 1) % NYA) * NZA + za), dev(x=((ya + 3) % NYA) * NZA + za),
        dev(x=ya * NZA + (za + 1) % NZA), dev(x=ya * NZA + (za + 7) % NZA),
    )
    greet(dev(g=1 - grp))
    for device in ring:
        greet(device)
    wrap_left = (za == 0) & has_left
    wrap_right = (za == NZA - 1) & has_right

    @pl.when(wrap_left)
    def _():
        greet(dev(x=tx - 1))

    @pl.when(wrap_right)
    def _():
        greet(dev(x=tx + 1))

    def vouch(stage, sides):
        for side in sides:
            pl.semaphore_signal(
                far_sem.at[stage, side], inc=1, device_id=ring[side], device_id_type=MESH
            )

    def vouched(stage, sides):
        for side in sides:
            pl.semaphore_wait(far_sem.at[stage, side], 1)

    for copy in smalls:
        copy.wait()
    oa[:, 0:SLOTS] = obs[...].T
    lane = lax.broadcasted_iota(jnp.int32, (NL, 128), 1)
    scale = jnp.where(child, 3, 1)
    off = jnp.where(child, 0, nest_y[0])

    def selection(shape, ydim):
        d = lax.broadcasted_iota(jnp.int32, shape, ydim)
        d = d - scale * lax.broadcasted_iota(jnp.int32, shape, 1 - ydim) - off
        return jnp.where((d >= 0) & (d < scale), 1.0, 0.0).astype(BF16)

    wsel[0:NYC] = selection((NYC, 128), 0)
    wsel[NYC:] = wsel[0:NYC]
    wback[0:128] = selection((128, NYC), 1)
    wback[128:] = wback[0:128]
    mc[...] = jnp.zeros_like(mc)
    xs[...] = jnp.zeros_like(xs)
    xe[...] = jnp.zeros_like(xe)
    for f in range(NF):
        high, low = split(mix[f, :, 0, :])
        mc[f, 0:NL, 0:NL] = high
        mc[f, 0:NL, 64:64 + NL] = high
        mc[f, 0:NL, 128:128 + NL] = low
    cu[4] = jnp.zeros(cu.shape[1:], F32)

    @pl.when(tx == 0)
    def _():
        for f in range(NF):
            ms[f, 0] = jnp.zeros(ms.shape[2:], F32)

    @pl.when(tx == NTX - 1)
    def _():
        for f in range(NF):
            ms[f, NXC + 1] = jnp.zeros(ms.shape[2:], F32)

    @pl.when(ty == 0)
    def _():
        yhalo[0] = jnp.zeros(yhalo.shape[1:], F32)

    @pl.when(ty == NTY - 1)
    def _():
        yhalo[1] = jnp.zeros(yhalo.shape[1:], F32)

    def obs1(d):
        peer = (ty + d) % NTY
        return pltpu.make_async_remote_copy(
            oa.at[pl.ds(pl.multiple_of(peer * NTX, NTX), NTX)], ob.at[ty], os1.at[d - 1], or1.at[d - 1],
            device_id=dev(y=peer), device_id_type=MESH,
        )

    def obs2(d):
        peer = (ya + d) % NYA
        return pltpu.make_async_remote_copy(
            oc.at[pl.ds(pl.multiple_of(peer * NZA, NZA), NZA)],
            od.at[pl.ds(pl.multiple_of(ya * NZA, NZA), NZA)], os2.at[d - 1], or2.at[d - 1],
            device_id=dev(x=peer * NZA + za), device_id_type=MESH,
        )

    def obs3(d):
        peer = (za + d) % NZA
        return pltpu.make_async_remote_copy(
            oe.at[peer], og.at[za], os3.at[d - 1], or3.at[d - 1],
            device_id=dev(x=ya * NZA + peer), device_id_type=MESH,
        )

    def halo(f, side):
        source, target, x = (1, NXC + 1, tx - 1) if side == 0 else (NXC, 0, tx + 1)
        return pltpu.make_async_remote_copy(
            ms.at[f, source, :, pl.ds(0, NL)], ms.at[f, target, :, pl.ds(0, NL)], hs_sem.at[side, f], hr_sem.at[side, f],
            device_id=dev(x=x), device_id_type=MESH,
        )

    def send_halo(f):
        @pl.when(has_left)
        def _():
            halo(f, 0).start()

        @pl.when(has_right)
        def _():
            halo(f, 1).start()

    def ends(first, last, row, x):
        pair = jnp.where(row < 64, first, last)
        return pltpu.roll(pair, 2 * x, axis=1) if x else pair

    def planes(f, carry):
        fetch(f).wait()
        edge = jnp.zeros((NL, 128), F32)
        for x in range(NXC):
            value = []
            for b in range(NB):
                r = x * NB + b
                value.append(raw[f, pl.ds(r, NL, stride=STEP), :] * mask[r].astype(F32))
                ms[f, x + 1, b, 0:NL] = value[b]
            here = (lane == 2 * x) | (lane == (2 * x - 1) % 128)
            edge = jnp.where(here, ends(value[0], value[NB - 1], lane, x), edge)
        turned = pltpu.roll(edge, 2 * NXC * f, axis=1)
        return jnp.where(((lane + 1 - 2 * NXC * f) & 127) < 2 * NXC, turned, carry)

    ycols[0:NL] = lax.fori_loop(0, NF, planes, jnp.zeros((NL, 128), F32))

    def yedge(side):
        return pltpu.make_async_remote_copy(
            ycols.at[pl.ds(0, NL)], yhalo.at[1 - side, pl.ds(0, NL)], ys_sem.at[side], yr_sem.at[side],
            device_id=dev(y=ty - 1 if side == 0 else ty + 1), device_id_type=MESH,
        )

    pl.semaphore_wait(barrier, 1 + len(ring) + jnp.where(wrap_left | wrap_right, 1, 0))

    @pl.when(has_down)
    def _():
        yedge(0).start()

    @pl.when(has_up)
    def _():
        yedge(1).start()

    for f in range(AHEAD):
        send_halo(f)
    vouch(0, range(6))
    row = lax.broadcasted_iota(jnp.int32, (1, 128), 1)
    kends = jnp.zeros((1, 128), F32)
    for x in range(NXC):
        here = (row == 2 * x) | (row == (2 * x - 1) % 128)
        kends = jnp.where(here, ends(kappa[x * NB], kappa[x * NB + NB - 1], row, x), kends)

    def feedback(f, part):
        planes = pl.ds(2 * part, 2)
        return pltpu.make_async_remote_copy(
            pay.at[f, planes, pl.ds(0, NL)], got.at[f, planes, pl.ds(0, NL)],
            gs_sem.at[part, f], gr_sem.at[part, f],
            device_id=dev(g=1 - grp), device_id_type=MESH,
        )

    def keep(ref, i, value):
        high, low = split(value)
        width = value.shape[1]
        ref[i * 64:i * 64 + NL, 0:width] = high
        ref[i * 64:i * 64 + NL, width:2 * width] = low

    def fill(ref, start, stop, columns, value):
        high, low = split(value)
        n = stop - start
        ref[start:stop, columns] = high[0:n]
        ref[64 + start:64 + stop, columns] = low[0:n]
        ref[128 + start:128 + stop, columns] = high[0:n]

    lane16 = lax.broadcasted_iota(jnp.int32, (16, 128), 1)

    def stencil(f, xpair, pair):
        for start, size in ((0, 16), (16, 16), (32, 16), (48, 8)):
            rows = slice(start, start + size)
            lanes = lane16[0:size]
            for half, x in enumerate(xpair):
                cells = [ms[f, x + 1, b, rows] for b in range(NB)]
                up = [pltpu.roll(c, 1, axis=1) for c in cells]
                down = [pltpu.roll(c, 127, axis=1) for c in cells]
                for b in range(NB):
                    prev = jnp.where(lanes == 0, up[b - 1] if b else 0.0, up[b])
                    after = jnp.where(lanes == 127, down[b + 1] if b < NB - 1 else 0.0, down[b])
                    beside = ms[f, x, b, rows] + ms[f, x + 2, b, rows] + prev + after
                    spread = cells[b] + kappa[x * NB + b] * (beside - 4.0 * cells[b])
                    col = half * NYC + b * 128
                    fill(xs.at[pair], start, min(start + size, NL), slice(col, col + 128), spread)

    def mix_ends(f):
        even = (lane & 1) == 0
        outer = jnp.where(
            even, pltpu.roll(yhalo[0, 0:NL], 1, axis=1), pltpu.roll(yhalo[1, 0:NL], 127, axis=1)
        )
        outer = pltpu.roll(outer, lax.rem(256 - 2 * NXC * f, 128), axis=1) * kends
        fill(xe, 0, NL, slice(0, 128), outer)
        em[f] = jnp.dot(mc[f], xe[...], preferred_element_type=F32)[0:LP]

    def add_ends(f, x):
        term = em[f, 0:NL]
        term = pltpu.roll(term, 128 - 2 * x, axis=1) if x else term
        mx[f, x, 0:NL, 0:128] += jnp.where(lane == 0, term, 0.0)
        mx[f, x, 0:NL, NYC - 128:] += jnp.where(lane == 127, term, 0.0)

    def blend(f, pair, x0, x1):
        mixed = jnp.dot(mc[f], xs[pair], preferred_element_type=F32)
        mx[f, x0] = mixed[0:LP, 0:NYC]
        mx[f, x1] = mixed[0:LP, NYC:]

    groups = ((1, 2), (0, 3))

    def give_back(f, part):
        @pl.when(child)
        def _():
            for n, i in enumerate(groups[part]):
                total = mx[f, 3 * i, 0:NL] * nudge[3 * i:3 * i + 1, :]
                for a in range(1, 3):
                    total = total + mx[f, 3 * i + a, 0:NL] * nudge[3 * i + a:3 * i + a + 1, :]
                keep(lhs, n, total)

        @pl.when(parent)
        def _():
            for n, i in enumerate(groups[part]):
                keep(lhs, n, mx[f, nest_x[0] + i, 0:NL])

        picked = jnp.dot(lhs[...], wsel[...], preferred_element_type=F32)
        for n in range(2):
            pay[f, 2 * part + n, 0:NL] = picked[n * 64:n * 64 + NL]
        feedback(f, part).start()

    def ready(f):
        mix_ends(f)
        for x in range(1, NXC - 1):
            add_ends(f, x)
        give_back(f, 0)

    def interior(f, carry):
        @pl.when(f + AHEAD < NF)
        def _():
            send_halo(f + AHEAD)

        for pair in range(NXC // 2 - 1):
            stencil(f, (2 * pair + 1, 2 * pair + 2), pair)
            blend(f, pair, 2 * pair + 1, 2 * pair + 2)

        @pl.when(f == 1)
        def _():
            @pl.when(has_down)
            def _():
                yedge(1).wait_recv()

            @pl.when(has_up)
            def _():
                yedge(0).wait_recv()

        @pl.when(f > 0)
        def _():
            ready(f - 1)

        return carry

    lax.fori_loop(0, NF, interior, 0)
    ready(NF - 1)

    vouched(0, range(6))
    vouch(1, (4, 5))
    for d in range(1, NTY):
        obs1(d).start()

    def border(f, carry):
        @pl.when(has_left)
        def _():
            halo(f, 1).wait_recv()

        @pl.when(has_right)
        def _():
            halo(f, 0).wait_recv()

        stencil(f, (0, NXC - 1), NXC // 2 - 1)
        blend(f, NXC // 2 - 1, 0, NXC - 1)
        add_ends(f, 0)
        add_ends(f, NXC - 1)
        give_back(f, 1)

        @pl.when(f == 1)
        def _():
            vouched(1, (4, 5))
            vouch(2, (4, 5))
            for d in range(1, NTY):
                obs1(d).wait_recv()
            ob[ty] = oa[pl.ds(pl.multiple_of(ty * NTX, NTX), NTX), :]
            for s in range(NTY):
                oc[:, s * SLOTS:(s + 1) * SLOTS] = ob[s, :, 0:SLOTS]
            for d in range(1, NYA):
                obs2(d).start()

        @pl.when(f == 3)
        def _():
            vouched(2, (4, 5))
            for d in range(1, NYA):
                obs2(d).wait_recv()
            own = pl.ds(pl.multiple_of(ya * NZA, NZA), NZA)
            od[own, :] = oc[own, :]
            for z in range(NZA):
                oe[z, 0:NYA] = od[pl.ds(z, NYA, stride=NZA), :]
            for d in range(1, NZA):
                obs3(d).start()

        return carry

    lax.fori_loop(0, NF, border, 0)

    take = jnp.where(child, 1.0 / 9.0, 1.0)
    give = jnp.where(child, 0.0, 1.0)

    def finish(f, carry):
        for part in range(2):
            feedback(f, part).wait_recv()
        for i in range(4):
            keep(dlt, i, got[f, i, 0:NL] * take - pay[f, i, 0:NL] * give)
        laid = jnp.dot(dlt[...], wback[...], preferred_element_type=F32)
        for n, i in enumerate(groups[0] + groups[1]):
            cu[i, 0:NL] = laid[n * 64:n * 64 + NL]
        for x in range(NXC):
            p = x - nest_x[0]
            index = jnp.where(child, x // 3, jnp.where((p >= 0) & (p < 4), p, 4))
            done = mx[f, x, 0:NL] + cu[index, 0:NL]
            for b in range(NB):
                raw[f, pl.ds(x * NB + b, NL, stride=STEP), :] = done[:, b * 128:(b + 1) * 128]
        leave(f).start()
        return carry

    def leave(f):
        return pltpu.make_async_copy(raw.at[f], out.at[f], out_sem.at[f])

    lax.fori_loop(0, NF, finish, 0)

    for d in range(1, NZA):
        obs3(d).wait_recv()
    og[za] = oe[za]
    for z in range(NZA):
        packed[z * 8:(z + 1) * 8, :] = og[z]
    leave_obs = pltpu.make_async_copy(packed, obs_out, out_sem.at[NF])
    leave_obs.start()

    for d in range(1, NTY):
        obs1(d).wait_send()
    for d in range(1, NYA):
        obs2(d).wait_send()
    for d in range(1, NZA):
        obs3(d).wait_send()

    @pl.when(has_left)
    def _():
        for f in range(NF):
            halo(f, 0).wait_send()

    @pl.when(has_right)
    def _():
        for f in range(NF):
            halo(f, 1).wait_send()

    @pl.when(has_down)
    def _():
        yedge(0).wait_send()

    @pl.when(has_up)
    def _():
        yedge(1).wait_send()

    for f in range(NF):
        for part in range(2):
            feedback(f, part).wait_send()
        leave(f).wait()
    leave_obs.wait()


def scatter_kernel(
    vals_in, cells_in, counts_in, start_in, mask_in,
    out, vals, cells, counts, start, mask, terms, wide, index, add0, add1, in_sem, out_sem,
):
    fetches = [
        pltpu.make_async_copy(source, target, in_sem.at[i])
        for i, (source, target) in enumerate(
            [(vals_in, vals), (cells_in, cells), (counts_in, counts), (mask_in, mask), (cells_in, index), (start_in, start)]
        )
    ]
    for fetch in fetches:
        fetch.start()
    add0[...] = jnp.zeros_like(add0)
    add1[...] = jnp.zeros_like(add1)
    for fetch in fetches[:5]:
        fetch.wait()
    for r in range(2 * STEP):
        wide[r:r + 1, :] = mask[r % STEP].astype(F32)
    slot = lax.broadcasted_iota(jnp.int32, (SLOTS, 128), 0)
    lane = lax.broadcasted_iota(jnp.int32, (SLOTS, 128), 1)
    lanes = jnp.where(slot < counts[...], cells[...] & 127, -1)
    turned = vals[...].T
    for s in range(NTY * NTX):
        t, y, z = s // NTX, s % NTX // NZA, s % NZA
        value = turned[t * SLOTS:(t + 1) * SLOTS, z * 8 + y:z * 8 + y + 1]
        terms[s * SLOTS:(s + 1) * SLOTS, :] = jnp.where(lane == lanes[:, s:s + 1], value, 0.0)

    def source(s, carry):
        for k in range(SLOTS):
            row = pl.ds(lax.shift_right_logical(index[k, s], 7), 1)
            ref = add1 if k % 2 else add0
            ref[row, :] = ref[row, :] + terms[pl.ds(s * SLOTS + k, 1), :]
        return carry

    lax.fori_loop(0, NTY * NTX, source, 0)
    fetches[5].wait()

    def leave(f):
        rows = pl.ds(f * ROWS, ROWS)
        return pltpu.make_async_copy(add0.at[rows], out.at[rows], out_sem.at[f])

    for f in range(NF):
        def masked(i, carry):
            rows = pl.ds(pl.multiple_of(f * ROWS + i * 2 * STEP, 8), 2 * STEP)
            add0[rows, :] = wide[...] * (start[rows, :] + add0[rows, :] + add1[rows, :])
            return carry

        lax.fori_loop(0, ROWS // (2 * STEP), masked, 0)
        leave(f).start()
    for f in range(NF):
        leave(f).wait()


HBM = pl.BlockSpec(memory_space=pltpu.HBM)
DMA = pltpu.SemaphoreType.DMA


def local(
    adjoint_state, land_mask, diffusivity, mixing, nudging, nest_x, nest_y, obs_forcing, obs_cell, obs_count
):
    state = adjoint_state.reshape(NF, ROWS, 128)
    mask = land_mask.reshape(STEP, 1, 128)
    kappa = diffusivity.reshape(STEP, 1, 128)
    cells = jnp.transpose(obs_cell[0, :, :, 0])
    counts = obs_count[0, :, 0].reshape(1, -1)
    scratch = [
        pltpu.SMEM((1,), jnp.int32),
        pltpu.SMEM((1,), jnp.int32),
        pltpu.VMEM((STEP, 1, 128), jnp.int32),
        pltpu.VMEM((STEP, 1, 128), F32),
        pltpu.VMEM((NXC, NYC), F32),
        pltpu.VMEM((NF, NL, 1, NL), F32),
        pltpu.VMEM((SLOTS, 128), F32),
        pltpu.VMEM((NZA * 8, 128), F32),
        pltpu.VMEM((NF, ROWS, 128), F32),
        pltpu.VMEM((NF, NXC + 2, NB, LP, 128), F32),
        pltpu.VMEM((NXC // 2, 192, 2 * NYC), BF16),
        pltpu.VMEM((192, 128), BF16),
        pltpu.VMEM((NF, LP, 128), F32),
        pltpu.VMEM((NF, 64, 192), BF16),
        pltpu.VMEM((NF, NXC, LP, NYC), F32),
        pltpu.VMEM((2 * NYC, 128), BF16),
        pltpu.VMEM((256, NYC), BF16),
        pltpu.VMEM((128, 2 * NYC), BF16),
        pltpu.VMEM((NF, 4, LP, 128), F32),
        pltpu.VMEM((NF, 4, LP, 128), F32),
        pltpu.VMEM((256, 256), BF16),
        pltpu.VMEM((5, LP, NYC), F32),
        pltpu.VMEM((LP, 128), F32),
        pltpu.VMEM((2, LP, 128), F32),
        pltpu.VMEM((128, 128), F32),
        pltpu.VMEM((NTY, NTX, 128), F32),
        pltpu.VMEM((NTX, 128), F32),
        pltpu.VMEM((NTX, 128), F32),
        pltpu.VMEM((NZA, 8, 128), F32),
        pltpu.VMEM((NZA, 8, 128), F32),
        DMA((NF,)), DMA((2, NF)), DMA((2, NF)), DMA((2,)), DMA((2,)), DMA((2, NF)), DMA((2, NF)),
        DMA((NTY - 1,)), DMA((NTY - 1,)), DMA((NYA - 1,)), DMA((NYA - 1,)), DMA((NZA - 1,)), DMA((NZA - 1,)),
        DMA((7,)), pltpu.SemaphoreType.REGULAR((3, 6)), DMA((NF + 1,)),
    ]
    partial, arrived = pl.pallas_call(
        exchange_kernel,
        out_shape=(
            jax.ShapeDtypeStruct((NF, ROWS, 128), F32),
            jax.ShapeDtypeStruct((NZA * 8, 128), F32),
        ),
        in_specs=[HBM] * 8,
        out_specs=(HBM, HBM),
        scratch_shapes=scratch,
        compiler_params=pltpu.CompilerParams(
            collective_id=0, has_side_effects=True, vmem_limit_bytes=VMEM_BYTES
        ),
        name="exchange",
    )(nest_x, nest_y, state, mask, kappa, nudging, mixing.reshape(NF, NL, 1, NL), obs_forcing[0, 0])
    total = NF * ROWS
    result = pl.pallas_call(
        scatter_kernel,
        out_shape=jax.ShapeDtypeStruct((total, 128), F32),
        in_specs=[HBM] * 5,
        out_specs=HBM,
        scratch_shapes=[
            pltpu.VMEM((NZA * 8, 128), F32), pltpu.VMEM((SLOTS, NTY * NTX), jnp.int32),
            pltpu.VMEM((1, NTY * NTX), jnp.int32), pltpu.VMEM((total, 128), F32), pltpu.VMEM((STEP, 1, 128), jnp.int32),
            pltpu.VMEM((NTY * NTX * SLOTS, 128), F32), pltpu.VMEM((2 * STEP, 128), F32),
            pltpu.SMEM((SLOTS, NTY * NTX), jnp.int32),
            pltpu.VMEM((total, 128), F32), pltpu.VMEM((total, 128), F32), DMA((6,)), DMA((NF,)),
        ],
        compiler_params=pltpu.CompilerParams(vmem_limit_bytes=VMEM_BYTES),
        name="scatter",
    )(arrived, cells, counts, partial.reshape(total, 128), mask)
    return result.reshape(1, NF, NL, NXC, NYC)


def solution(mesh):
    in_specs = (
        P("grp", None, None, "tx", "ty"),
        P("grp", "tx", "ty"),
        P("grp", "tx", "ty"),
        P("grp", None, None, None),
        P("tx", "ty"),
        P(("ty", "tx")),
        P(("ty", "tx")),
        P("grp", ("ty", "tx"), None, None),
        P("grp", None, None, ("ty", "tx")),
        P("grp", None, ("ty", "tx")),
    )
    out_specs = P("grp", None, None, "tx", "ty")
    return jax.shard_map(local, mesh=mesh, in_specs=in_specs, out_specs=out_specs, check_vma=False)
```

```python
import functools

import jax
import jax.numpy as jnp
from jax import lax
from jax.experimental import pallas as pl
from jax.experimental.pallas import tpu as pltpu
from jax.sharding import PartitionSpec as P

MESH = pl.DeviceIdType.MESH
F32 = jnp.float32
BF16 = jnp.bfloat16
NF, NL, NXC, NYC = 5, 50, 12, 384
LP = 56
NB = NYC // 128
ROWS = NL * NXC * NB
STEP = NXC * NB
NTY, NTX, NYA, NZA = 4, 32, 4, 8
SLOTS = 16
AHEAD = 2
VMEM_BYTES = 63 * 2**20


def split(value):
    high = value.astype(BF16)
    low = (value - high.astype(F32)).astype(BF16)
    return high, low


def exchange_kernel(
    nest_x_in, nest_y_in, state, mask_in, kappa_in, nudge_in, mix_in, obs_in,
    out, obs_out,
    nest_x, nest_y, mask, kappa, nudge, mix, obs, packed,
    raw, ms, xs, mc, mx, wsel, wback, lhs, pay, got, dlt, cu,
    ycols, yhalo, outer, oa, ob, oc, od, oe, og,
    in_sem, hs_sem, hr_sem, ys_sem, yr_sem, gs_sem, gr_sem,
    os1, or1, os2, or2, os3, or3, small_sem, far_sem, out_sem,
):
    grp = lax.axis_index("grp")
    ty = lax.axis_index("ty")
    tx = lax.axis_index("tx")
    ya, za = tx // NZA, tx % NZA
    child = grp == 0
    parent = grp == 1

    def dev(g=None, y=None, x=None):
        return (grp if g is None else g, ty if y is None else y, tx if x is None else x)

    def fetch(f):
        return pltpu.make_async_copy(state.at[f], raw.at[f], in_sem.at[f])

    smalls = [
        pltpu.make_async_copy(source, target, small_sem.at[i])
        for i, (source, target) in enumerate(
            [(obs_in, obs), (mask_in, mask), (mix_in, mix), (nest_x_in, nest_x), (nest_y_in, nest_y),
             (kappa_in, kappa), (nudge_in, nudge)]
        )
    ]
    smalls[0].start()
    smalls[1].start()
    for f in range(NF):
        fetch(f).start()
    for copy in smalls[2:]:
        copy.start()

    barrier = pltpu.get_barrier_semaphore()

    def greet(target):
        pl.semaphore_signal(barrier, inc=1, device_id=target, device_id_type=MESH)

    has_left, has_right = tx > 0, tx < NTX - 1
    has_down, has_up = ty > 0, ty < NTY - 1
    ring = (
        dev(y=(ty + 1) % NTY), dev(y=(ty + 3) % NTY),
        dev(x=((ya + 1) % NYA) * NZA + za), dev(x=((ya + 3) % NYA) * NZA + za),
        dev(x=ya * NZA + (za + 1) % NZA), dev(x=ya * NZA + (za + 7) % NZA),
    )
    greet(dev(g=1 - grp))
    for device in ring:
        greet(device)
    wrap_left = (za == 0) & has_left
    wrap_right = (za == NZA - 1) & has_right

    @pl.when(wrap_left)
    def _():
        greet(dev(x=tx - 1))

    @pl.when(wrap_right)
    def _():
        greet(dev(x=tx + 1))

    def vouch(stage, sides):
        for side in sides:
            pl.semaphore_signal(
                far_sem.at[stage, side], inc=1, device_id=ring[side], device_id_type=MESH
            )

    def vouched(stage, sides):
        for side in sides:
            pl.semaphore_wait(far_sem.at[stage, side], 1)

    for copy in smalls:
        copy.wait()
    oa[:, 0:SLOTS] = obs[...].T
    lane = lax.broadcasted_iota(jnp.int32, (NL, 128), 1)
    scale = jnp.where(child, 3, 1)
    off = jnp.where(child, 0, nest_y[0])

    def selection(shape, ydim):
        d = lax.broadcasted_iota(jnp.int32, shape, ydim)
        d = d - scale * lax.broadcasted_iota(jnp.int32, shape, 1 - ydim) - off
        return jnp.where((d >= 0) & (d < scale), 1.0, 0.0).astype(BF16)

    wsel[0:NYC] = selection((NYC, 128), 0)
    wsel[NYC:] = wsel[0:NYC]
    wback[0:128] = selection((128, NYC), 1)
    wback[128:] = wback[0:128]
    mc[...] = jnp.zeros_like(mc)
    xs[...] = jnp.zeros_like(xs)
    for f in range(NF):
        high, low = split(mix[f, :, 0, :])
        mc[f, 0:NL, 0:NL] = high
        mc[f, 0:NL, 64:64 + NL] = high
        mc[f, 0:NL, 128:128 + NL] = low
    cu[4] = jnp.zeros(cu.shape[1:], F32)

    @pl.when(tx == 0)
    def _():
        for f in range(NF):
            ms[f, 0] = jnp.zeros(ms.shape[2:], F32)

    @pl.when(tx == NTX - 1)
    def _():
        for f in range(NF):
            ms[f, NXC + 1] = jnp.zeros(ms.shape[2:], F32)

    @pl.when(ty == 0)
    def _():
        yhalo[0] = jnp.zeros(yhalo.shape[1:], F32)

    @pl.when(ty == NTY - 1)
    def _():
        yhalo[1] = jnp.zeros(yhalo.shape[1:], F32)

    def obs1(d):
        peer = (ty + d) % NTY
        return pltpu.make_async_remote_copy(
            oa.at[pl.ds(pl.multiple_of(peer * NTX, NTX), NTX)], ob.at[ty], os1.at[d - 1], or1.at[d - 1],
            device_id=dev(y=peer), device_id_type=MESH,
        )

    def obs2(d):
        peer = (ya + d) % NYA
        return pltpu.make_async_remote_copy(
            oc.at[pl.ds(pl.multiple_of(peer * NZA, NZA), NZA)],
            od.at[pl.ds(pl.multiple_of(ya * NZA, NZA), NZA)], os2.at[d - 1], or2.at[d - 1],
            device_id=dev(x=peer * NZA + za), device_id_type=MESH,
        )

    def obs3(d):
        peer = (za + d) % NZA
        return pltpu.make_async_remote_copy(
            oe.at[peer], og.at[za], os3.at[d - 1], or3.at[d - 1],
            device_id=dev(x=ya * NZA + peer), device_id_type=MESH,
        )

    def halo(f, side):
        source, target, x = (1, NXC + 1, tx - 1) if side == 0 else (NXC, 0, tx + 1)
        return pltpu.make_async_remote_copy(
            ms.at[f, source, :, pl.ds(0, NL)], ms.at[f, target, :, pl.ds(0, NL)], hs_sem.at[side, f], hr_sem.at[side, f],
            device_id=dev(x=x), device_id_type=MESH,
        )

    def send_halo(f):
        @pl.when(has_left)
        def _():
            halo(f, 0).start()

        @pl.when(has_right)
        def _():
            halo(f, 1).start()

    def meet():
        pl.semaphore_wait(barrier, 1 + len(ring) + jnp.where(wrap_left | wrap_right, 1, 0))
        vouch(0, range(6))

    @pl.when(za != 0)
    def _():
        meet()

    def planes(f, carry):
        fetch(f).wait()
        edge = jnp.zeros((NL, 128), F32)
        for x in range(NXC):
            value = []
            for b in range(NB):
                r = x * NB + b
                value.append(raw[f, pl.ds(r, NL, stride=STEP), :] * mask[r].astype(F32))
                ms[f, x + 1, b, 0:NL] = value[b]
            pair = jnp.where(lane < 64, value[0], value[NB - 1])
            here = (lane == 2 * x) | (lane == (2 * x - 1) % 128)
            edge = jnp.where(here, pltpu.roll(pair, 2 * x, axis=1) if x else pair, edge)

        @pl.when((f < AHEAD) & (za != 0))
        def _():
            send_halo(f)

        turned = pltpu.roll(edge, 2 * NXC * f, axis=1)
        return jnp.where(((lane + 1 - 2 * NXC * f) & 127) < 2 * NXC, turned, carry)

    ycols[0:NL] = lax.fori_loop(0, NF, planes, jnp.zeros((NL, 128), F32))

    def yedge(side):
        return pltpu.make_async_remote_copy(
            ycols.at[pl.ds(0, NL)], yhalo.at[1 - side, pl.ds(0, NL)], ys_sem.at[side], yr_sem.at[side],
            device_id=dev(y=ty - 1 if side == 0 else ty + 1), device_id_type=MESH,
        )

    @pl.when(za == 0)
    def _():
        meet()
        for f in range(AHEAD):
            send_halo(f)

    @pl.when(has_down)
    def _():
        yedge(0).start()

    @pl.when(has_up)
    def _():
        yedge(1).start()

    vouched(0, range(6))
    vouch(1, (4, 5))
    for d in range(1, NTY):
        obs1(d).start()

    @pl.when(has_down)
    def _():
        yedge(1).wait_recv()

    @pl.when(has_up)
    def _():
        yedge(0).wait_recv()

    even = (lane & 1) == 0
    outer[0:NL] = jnp.where(
        even, pltpu.roll(yhalo[0, 0:NL], 1, axis=1), pltpu.roll(yhalo[1, 0:NL], 127, axis=1)
    )

    def feedback(f):
        return pltpu.make_async_remote_copy(
            pay.at[f, :, pl.ds(0, NL)], got.at[f, :, pl.ds(0, NL)], gs_sem.at[f], gr_sem.at[f],
            device_id=dev(g=1 - grp), device_id_type=MESH,
        )

    def keep(ref, i, value):
        high, low = split(value)
        width = value.shape[1]
        ref[i * 64:i * 64 + NL, 0:width] = high
        ref[i * 64:i * 64 + NL, width:2 * width] = low

    lane16 = lax.broadcasted_iota(jnp.int32, (16, 128), 1)

    def stencil(f, pair, local):
        for start, size in ((0, 16), (16, 16), (32, 16), (48, 8)):
            rows = slice(start, start + size)
            keep_rows = min(size, NL - start)
            lanes = lane16[0:size]
            for half in range(2):
                x = 2 * pair + half
                cells = [ms[f, x + 1, b, rows] for b in range(NB)]
                edge = pltpu.roll(local[rows], 128 - 2 * x, axis=1) if x else local[rows]
                up = [pltpu.roll(c, 1, axis=1) for c in cells]
                down = [pltpu.roll(c, 127, axis=1) for c in cells]
                for b in range(NB):
                    prev = jnp.where(lanes == 0, up[b - 1] if b else edge, up[b])
                    after = jnp.where(lanes == 127, down[b + 1] if b < NB - 1 else edge, down[b])
                    beside = ms[f, x, b, rows] + ms[f, x + 2, b, rows] + prev + after
                    spread = cells[b] + kappa[x * NB + b] * (beside - 4.0 * cells[b])
                    high, low = split(spread)
                    columns = slice(half * NYC + b * 128, half * NYC + b * 128 + 128)
                    xs[pair, start:start + keep_rows, columns] = high[0:keep_rows]
                    xs[pair, 64 + start:64 + start + keep_rows, columns] = low[0:keep_rows]
                    xs[pair, 128 + start:128 + start + keep_rows, columns] = high[0:keep_rows]

    def advance(f, carry):
        @pl.when(f + AHEAD < NF)
        def _():
            send_halo(f + AHEAD)

        @pl.when(has_left)
        def _():
            halo(f, 1).wait_recv()

        @pl.when(has_right)
        def _():
            halo(f, 0).wait_recv()

        local = pltpu.roll(outer[...], lax.rem(256 - 2 * NXC * f, 128), axis=1)
        for pair in range(NXC // 2):
            stencil(f, pair, local)
            mixed = jnp.dot(mc[f], xs[pair], preferred_element_type=F32)
            mx[f, 2 * pair] = mixed[0:LP, 0:NYC]
            mx[f, 2 * pair + 1] = mixed[0:LP, NYC:]

        @pl.when(child)
        def _():
            for i in range(4):
                total = mx[f, 3 * i, 0:NL] * nudge[3 * i:3 * i + 1, :]
                for a in range(1, 3):
                    total = total + mx[f, 3 * i + a, 0:NL] * nudge[3 * i + a:3 * i + a + 1, :]
                keep(lhs, i, total)

        @pl.when(parent)
        def _():
            for i in range(4):
                keep(lhs, i, mx[f, nest_x[0] + i, 0:NL])

        picked = jnp.dot(lhs[...], wsel[...], preferred_element_type=F32)
        for i in range(4):
            pay[f, i, 0:NL] = picked[i * 64:i * 64 + NL]
        feedback(f).start()

        @pl.when(f == 0)
        def _():
            vouched(1, (4, 5))
            vouch(2, (4, 5))
            for d in range(1, NTY):
                obs1(d).wait_recv()
            ob[ty] = oa[pl.ds(pl.multiple_of(ty * NTX, NTX), NTX), :]
            for s in range(NTY):
                oc[:, s * SLOTS:(s + 1) * SLOTS] = ob[s, :, 0:SLOTS]
            for d in range(1, NYA):
                obs2(d).start()

        @pl.when(f == 2)
        def _():
            vouched(2, (4, 5))
            for d in range(1, NYA):
                obs2(d).wait_recv()
            own = pl.ds(pl.multiple_of(ya * NZA, NZA), NZA)
            od[own, :] = oc[own, :]
            for z in range(NZA):
                oe[z, 0:NYA] = od[pl.ds(z, NYA, stride=NZA), :]
            for d in range(1, NZA):
                obs3(d).start()

        return carry

    lax.fori_loop(0, NF, advance, 0)

    take = jnp.where(child, 1.0 / 9.0, 1.0)
    give = jnp.where(child, 0.0, 1.0)

    def finish(f, carry):
        feedback(f).wait_recv()
        for i in range(4):
            keep(dlt, i, got[f, i, 0:NL] * take - pay[f, i, 0:NL] * give)
        laid = jnp.dot(dlt[...], wback[...], preferred_element_type=F32)
        for i in range(4):
            cu[i, 0:NL] = laid[i * 64:i * 64 + NL]
        for x in range(NXC):
            p = x - nest_x[0]
            index = jnp.where(child, x // 3, jnp.where((p >= 0) & (p < 4), p, 4))
            done = mx[f, x, 0:NL] + cu[index, 0:NL]
            for b in range(NB):
                raw[f, pl.ds(x * NB + b, NL, stride=STEP), :] = done[:, b * 128:(b + 1) * 128]
        leave(f).start()
        return carry

    def leave(f):
        return pltpu.make_async_copy(raw.at[f], out.at[f], out_sem.at[f])

    lax.fori_loop(0, NF, finish, 0)

    for d in range(1, NZA):
        obs3(d).wait_recv()
    og[za] = oe[za]
    for z in range(NZA):
        packed[z * 8:(z + 1) * 8, :] = og[z]
    leave_obs = pltpu.make_async_copy(packed, obs_out, out_sem.at[NF])
    leave_obs.start()

    for d in range(1, NTY):
        obs1(d).wait_send()
    for d in range(1, NYA):
        obs2(d).wait_send()
    for d in range(1, NZA):
        obs3(d).wait_send()

    @pl.when(has_left)
    def _():
        for f in range(NF):
            halo(f, 0).wait_send()

    @pl.when(has_right)
    def _():
        for f in range(NF):
            halo(f, 1).wait_send()

    @pl.when(has_down)
    def _():
        yedge(0).wait_send()

    @pl.when(has_up)
    def _():
        yedge(1).wait_send()

    for f in range(NF):
        feedback(f).wait_send()
        leave(f).wait()
    leave_obs.wait()


def scatter_kernel(
    vals_in, cells_in, counts_in, start_in, mask_in,
    out, vals, cells, counts, start, mask, terms, wide, index, add0, add1, in_sem, out_sem,
):
    fetches = [
        pltpu.make_async_copy(source, target, in_sem.at[i])
        for i, (source, target) in enumerate(
            [(vals_in, vals), (cells_in, cells), (counts_in, counts), (mask_in, mask), (cells_in, index), (start_in, start)]
        )
    ]
    for fetch in fetches:
        fetch.start()
    add0[...] = jnp.zeros_like(add0)
    add1[...] = jnp.zeros_like(add1)
    for fetch in fetches[:5]:
        fetch.wait()
    for r in range(2 * STEP):
        wide[r:r + 1, :] = mask[r % STEP].astype(F32)
    slot = lax.broadcasted_iota(jnp.int32, (SLOTS, 128), 0)
    lane = lax.broadcasted_iota(jnp.int32, (SLOTS, 128), 1)
    lanes = jnp.where(slot < counts[...], cells[...] & 127, -1)
    turned = vals[...].T
    for s in range(NTY * NTX):
        t, y, z = s // NTX, s % NTX // NZA, s % NZA
        value = turned[t * SLOTS:(t + 1) * SLOTS, z * 8 + y:z * 8 + y + 1]
        terms[s * SLOTS:(s + 1) * SLOTS, :] = jnp.where(lane == lanes[:, s:s + 1], value, 0.0)

    def source(i, carry):
        for u in range(4):
            s = i * 4 + u
            for k in range(SLOTS):
                row = pl.ds(lax.shift_right_logical(index[k, s], 7), 1)
                ref = add1 if k % 2 else add0
                ref[row, :] = ref[row, :] + terms[pl.ds(s * SLOTS + k, 1), :]
        return carry

    lax.fori_loop(0, NTY * NTX // 4, source, 0)
    fetches[5].wait()

    def leave(f):
        rows = pl.ds(f * ROWS, ROWS)
        return pltpu.make_async_copy(add0.at[rows], out.at[rows], out_sem.at[f])

    for f in range(NF):
        def masked(i, carry):
            rows = pl.ds(pl.multiple_of(f * ROWS + i * 2 * STEP, 8), 2 * STEP)
            add0[rows, :] = wide[...] * (start[rows, :] + add0[rows, :] + add1[rows, :])
            return carry

        lax.fori_loop(0, ROWS // (2 * STEP), masked, 0)
        leave(f).start()
    for f in range(NF):
        leave(f).wait()


HBM = pl.BlockSpec(memory_space=pltpu.HBM)
DMA = pltpu.SemaphoreType.DMA


def local(
    adjoint_state, land_mask, diffusivity, mixing, nudging, nest_x, nest_y, obs_forcing, obs_cell, obs_count
):
    state = adjoint_state.reshape(NF, ROWS, 128)
    mask = land_mask.reshape(STEP, 1, 128)
    kappa = diffusivity.reshape(STEP, 1, 128)
    cells = jnp.transpose(obs_cell[0, :, :, 0])
    counts = obs_count[0, :, 0].reshape(1, -1)
    scratch = [
        pltpu.SMEM((1,), jnp.int32),
        pltpu.SMEM((1,), jnp.int32),
        pltpu.VMEM((STEP, 1, 128), jnp.int32),
        pltpu.VMEM((STEP, 1, 128), F32),
        pltpu.VMEM((NXC, NYC), F32),
        pltpu.VMEM((NF, NL, 1, NL), F32),
        pltpu.VMEM((SLOTS, 128), F32),
        pltpu.VMEM((NZA * 8, 128), F32),
        pltpu.VMEM((NF, ROWS, 128), F32),
        pltpu.VMEM((NF, NXC + 2, NB, LP, 128), F32),
        pltpu.VMEM((NXC // 2, 192, 2 * NYC), BF16),
        pltpu.VMEM((NF, 64, 192), BF16),
        pltpu.VMEM((NF, NXC, LP, NYC), F32),
        pltpu.VMEM((2 * NYC, 128), BF16),
        pltpu.VMEM((256, NYC), BF16),
        pltpu.VMEM((256, 2 * NYC), BF16),
        pltpu.VMEM((NF, 4, LP, 128), F32),
        pltpu.VMEM((NF, 4, LP, 128), F32),
        pltpu.VMEM((256, 256), BF16),
        pltpu.VMEM((5, LP, NYC), F32),
        pltpu.VMEM((LP, 128), F32),
        pltpu.VMEM((2, LP, 128), F32),
        pltpu.VMEM((LP, 128), F32),
        pltpu.VMEM((128, 128), F32),
        pltpu.VMEM((NTY, NTX, 128), F32),
        pltpu.VMEM((NTX, 128), F32),
        pltpu.VMEM((NTX, 128), F32),
        pltpu.VMEM((NZA, 8, 128), F32),
        pltpu.VMEM((NZA, 8, 128), F32),
        DMA((NF,)), DMA((2, NF)), DMA((2, NF)), DMA((2,)), DMA((2,)), DMA((NF,)), DMA((NF,)),
        DMA((NTY - 1,)), DMA((NTY - 1,)), DMA((NYA - 1,)), DMA((NYA - 1,)), DMA((NZA - 1,)), DMA((NZA - 1,)),
        DMA((7,)), pltpu.SemaphoreType.REGULAR((3, 6)), DMA((NF + 1,)),
    ]
    partial, arrived = pl.pallas_call(
        exchange_kernel,
        out_shape=(
            jax.ShapeDtypeStruct((NF, ROWS, 128), F32),
            jax.ShapeDtypeStruct((NZA * 8, 128), F32),
        ),
        in_specs=[HBM] * 8,
        out_specs=(HBM, HBM),
        scratch_shapes=scratch,
        compiler_params=pltpu.CompilerParams(
            collective_id=0, has_side_effects=True, vmem_limit_bytes=VMEM_BYTES
        ),
        name="exchange",
    )(nest_x, nest_y, state, mask, kappa, nudging, mixing.reshape(NF, NL, 1, NL), obs_forcing[0, 0])
    total = NF * ROWS
    result = pl.pallas_call(
        scatter_kernel,
        out_shape=jax.ShapeDtypeStruct((total, 128), F32),
        in_specs=[HBM] * 5,
        out_specs=HBM,
        scratch_shapes=[
            pltpu.VMEM((NZA * 8, 128), F32), pltpu.VMEM((SLOTS, NTY * NTX), jnp.int32),
            pltpu.VMEM((1, NTY * NTX), jnp.int32), pltpu.VMEM((total, 128), F32), pltpu.VMEM((STEP, 1, 128), jnp.int32),
            pltpu.VMEM((NTY * NTX * SLOTS, 128), F32), pltpu.VMEM((2 * STEP, 128), F32),
            pltpu.SMEM((SLOTS, NTY * NTX), jnp.int32),
            pltpu.VMEM((total, 128), F32), pltpu.VMEM((total, 128), F32), DMA((6,)), DMA((NF,)),
        ],
        compiler_params=pltpu.CompilerParams(vmem_limit_bytes=VMEM_BYTES),
        name="scatter",
    )(arrived, cells, counts, partial.reshape(total, 128), mask)
    return result.reshape(1, NF, NL, NXC, NYC)


def solution(mesh):
    in_specs = (
        P("grp", None, None, "tx", "ty"),
        P("grp", "tx", "ty"),
        P("grp", "tx", "ty"),
        P("grp", None, None, None),
        P("tx", "ty"),
        P(("ty", "tx")),
        P(("ty", "tx")),
        P("grp", ("ty", "tx"), None, None),
        P("grp", None, None, ("ty", "tx")),
        P("grp", None, ("ty", "tx")),
    )
    out_specs = P("grp", None, None, "tx", "ty")
    return jax.shard_map(local, mesh=mesh, in_specs=in_specs, out_specs=out_specs, check_vma=False)
```

```python
import functools

import jax
import jax.numpy as jnp
from jax import lax
from jax.experimental import pallas as pl
from jax.experimental.pallas import tpu as pltpu
from jax.sharding import PartitionSpec as P

MESH = pl.DeviceIdType.MESH
F32 = jnp.float32
BF16 = jnp.bfloat16
NF, NL, NXC, NYC = 5, 50, 12, 384
LP = 56
NB = NYC // 128
ROWS = NL * NXC * NB
STEP = NXC * NB
NTY, NTX, NYA, NZA = 4, 32, 4, 8
SLOTS = 16
AHEAD = 3
VMEM_BYTES = 63 * 2**20


def split(value):
    high = value.astype(BF16)
    low = (value - high.astype(F32)).astype(BF16)
    return high, low


def exchange_kernel(
    nest_x_in, nest_y_in, state, mask_in, kappa_in, nudge_in, mix_in, obs_in,
    out, obs_out,
    nest_x, nest_y, mask, kappa, nudge, mix, obs, packed,
    raw, ms, xs, mc, mx, wsel, wback, lhs, pay, got, dlt, cu,
    ycols, yhalo, outer, oa, ob, oc, od, oe, og,
    in_sem, hs_sem, hr_sem, ys_sem, yr_sem, gs_sem, gr_sem,
    os1, or1, os2, or2, os3, or3, small_sem, far_sem, out_sem,
):
    grp = lax.axis_index("grp")
    ty = lax.axis_index("ty")
    tx = lax.axis_index("tx")
    ya, za = tx // NZA, tx % NZA
    child = grp == 0
    parent = grp == 1

    def dev(g=None, y=None, x=None):
        return (grp if g is None else g, ty if y is None else y, tx if x is None else x)

    def fetch(f):
        return pltpu.make_async_copy(state.at[f], raw.at[f], in_sem.at[f])

    smalls = [
        pltpu.make_async_copy(source, target, small_sem.at[i])
        for i, (source, target) in enumerate(
            [(obs_in, obs), (mask_in, mask), (mix_in, mix), (nest_x_in, nest_x), (nest_y_in, nest_y),
             (kappa_in, kappa), (nudge_in, nudge)]
        )
    ]
    smalls[0].start()
    smalls[1].start()
    for f in range(NF):
        fetch(f).start()
    for copy in smalls[2:]:
        copy.start()

    barrier = pltpu.get_barrier_semaphore()

    def greet(target):
        pl.semaphore_signal(barrier, inc=1, device_id=target, device_id_type=MESH)

    has_left, has_right = tx > 0, tx < NTX - 1
    has_down, has_up = ty > 0, ty < NTY - 1
    ring = (
        dev(y=(ty + 1) % NTY), dev(y=(ty + 3) % NTY),
        dev(x=((ya + 1) % NYA) * NZA + za), dev(x=((ya + 3) % NYA) * NZA + za),
        dev(x=ya * NZA + (za + 1) % NZA), dev(x=ya * NZA + (za + 7) % NZA),
    )
    greet(dev(g=1 - grp))
    for device in ring:
        greet(device)
    wrap_left = (za == 0) & has_left
    wrap_right = (za == NZA - 1) & has_right

    @pl.when(wrap_left)
    def _():
        greet(dev(x=tx - 1))

    @pl.when(wrap_right)
    def _():
        greet(dev(x=tx + 1))

    def vouch(stage, sides):
        for side in sides:
            pl.semaphore_signal(
                far_sem.at[stage, side], inc=1, device_id=ring[side], device_id_type=MESH
            )

    def vouched(stage, sides):
        for side in sides:
            pl.semaphore_wait(far_sem.at[stage, side], 1)

    for copy in smalls:
        copy.wait()
    oa[:, 0:SLOTS] = obs[...].T
    lane = lax.broadcasted_iota(jnp.int32, (NL, 128), 1)
    scale = jnp.where(child, 3, 1)
    off = jnp.where(child, 0, nest_y[0])

    def selection(shape, ydim):
        d = lax.broadcasted_iota(jnp.int32, shape, ydim)
        d = d - scale * lax.broadcasted_iota(jnp.int32, shape, 1 - ydim) - off
        return jnp.where((d >= 0) & (d < scale), 1.0, 0.0).astype(BF16)

    wsel[0:NYC] = selection((NYC, 128), 0)
    wsel[NYC:] = wsel[0:NYC]
    wback[0:128] = selection((128, NYC), 1)
    wback[128:] = wback[0:128]
    mc[...] = jnp.zeros_like(mc)
    xs[...] = jnp.zeros_like(xs)
    for f in range(NF):
        high, low = split(mix[f, :, 0, :])
        mc[f, 0:NL, 0:NL] = high
        mc[f, 0:NL, 64:64 + NL] = high
        mc[f, 0:NL, 128:128 + NL] = low
    cu[4] = jnp.zeros(cu.shape[1:], F32)

    @pl.when(tx == 0)
    def _():
        for f in range(NF):
            ms[f, 0] = jnp.zeros(ms.shape[2:], F32)

    @pl.when(tx == NTX - 1)
    def _():
        for f in range(NF):
            ms[f, NXC + 1] = jnp.zeros(ms.shape[2:], F32)

    @pl.when(ty == 0)
    def _():
        yhalo[0] = jnp.zeros(yhalo.shape[1:], F32)

    @pl.when(ty == NTY - 1)
    def _():
        yhalo[1] = jnp.zeros(yhalo.shape[1:], F32)

    def obs1(d):
        peer = (ty + d) % NTY
        return pltpu.make_async_remote_copy(
            oa.at[pl.ds(pl.multiple_of(peer * NTX, NTX), NTX)], ob.at[ty], os1.at[d - 1], or1.at[d - 1],
            device_id=dev(y=peer), device_id_type=MESH,
        )

    def obs2(d):
        peer = (ya + d) % NYA
        return pltpu.make_async_remote_copy(
            oc.at[pl.ds(pl.multiple_of(peer * NZA, NZA), NZA)],
            od.at[pl.ds(pl.multiple_of(ya * NZA, NZA), NZA)], os2.at[d - 1], or2.at[d - 1],
            device_id=dev(x=peer * NZA + za), device_id_type=MESH,
        )

    def obs3(d):
        peer = (za + d) % NZA
        return pltpu.make_async_remote_copy(
            oe.at[peer], og.at[za], os3.at[d - 1], or3.at[d - 1],
            device_id=dev(x=ya * NZA + peer), device_id_type=MESH,
        )

    def halo(f, side):
        source, target, x = (1, NXC + 1, tx - 1) if side == 0 else (NXC, 0, tx + 1)
        return pltpu.make_async_remote_copy(
            ms.at[f, source, :, pl.ds(0, NL)], ms.at[f, target, :, pl.ds(0, NL)], hs_sem.at[side, f], hr_sem.at[side, f],
            device_id=dev(x=x), device_id_type=MESH,
        )

    def send_halo(f):
        @pl.when(has_right)
        def _():
            halo(f, 1).start()

        @pl.when(has_left)
        def _():
            halo(f, 0).start()

    def meet():
        pl.semaphore_wait(barrier, 1 + len(ring) + jnp.where(wrap_left | wrap_right, 1, 0))
        vouch(0, range(6))

    @pl.when(za != 0)
    def _():
        meet()

    def planes(f, carry):
        fetch(f).wait()
        edge = jnp.zeros((NL, 128), F32)
        for x in range(NXC):
            value = []
            for b in range(NB):
                r = x * NB + b
                value.append(raw[f, pl.ds(r, NL, stride=STEP), :] * mask[r].astype(F32))
                ms[f, x + 1, b, 0:NL] = value[b]
            pair = jnp.where(lane < 64, value[0], value[NB - 1])
            here = (lane == 2 * x) | (lane == (2 * x - 1) % 128)
            edge = jnp.where(here, pltpu.roll(pair, 2 * x, axis=1) if x else pair, edge)

        @pl.when((f < AHEAD) & (za != 0))
        def _():
            send_halo(f)

        turned = pltpu.roll(edge, 2 * NXC * f, axis=1)
        return jnp.where(((lane + 1 - 2 * NXC * f) & 127) < 2 * NXC, turned, carry)

    ycols[0:NL] = lax.fori_loop(0, NF, planes, jnp.zeros((NL, 128), F32))

    def yedge(side):
        return pltpu.make_async_remote_copy(
            ycols.at[pl.ds(0, NL)], yhalo.at[1 - side, pl.ds(0, NL)], ys_sem.at[side], yr_sem.at[side],
            device_id=dev(y=ty - 1 if side == 0 else ty + 1), device_id_type=MESH,
        )

    @pl.when(za == 0)
    def _():
        meet()
        for f in range(AHEAD):
            send_halo(f)

    @pl.when(has_down)
    def _():
        yedge(0).start()

    @pl.when(has_up)
    def _():
        yedge(1).start()

    vouched(0, range(6))
    vouch(1, (4, 5))
    for d in range(1, NTY):
        obs1(d).start()

    @pl.when(has_down)
    def _():
        yedge(1).wait_recv()

    @pl.when(has_up)
    def _():
        yedge(0).wait_recv()

    even = (lane & 1) == 0
    outer[0:NL] = jnp.where(
        even, pltpu.roll(yhalo[0, 0:NL], 1, axis=1), pltpu.roll(yhalo[1, 0:NL], 127, axis=1)
    )

    def feedback(f):
        return pltpu.make_async_remote_copy(
            pay.at[f, :, pl.ds(0, NL)], got.at[f, :, pl.ds(0, NL)], gs_sem.at[f], gr_sem.at[f],
            device_id=dev(g=1 - grp), device_id_type=MESH,
        )

    def keep(ref, i, value):
        high, low = split(value)
        width = value.shape[1]
        ref[i * 64:i * 64 + NL, 0:width] = high
        ref[i * 64:i * 64 + NL, width:2 * width] = low

    lane16 = lax.broadcasted_iota(jnp.int32, (16, 128), 1)

    def stencil(f, pair, local):
        for start, size in ((0, 16), (16, 16), (32, 16), (48, 8)):
            rows = slice(start, start + size)
            keep_rows = min(size, NL - start)
            lanes = lane16[0:size]
            for half in range(2):
                x = 2 * pair + half
                cells = [ms[f, x + 1, b, rows] for b in range(NB)]
                edge = pltpu.roll(local[rows], 128 - 2 * x, axis=1) if x else local[rows]
                up = [pltpu.roll(c, 1, axis=1) for c in cells]
                down = [pltpu.roll(c, 127, axis=1) for c in cells]
                for b in range(NB):
                    prev = jnp.where(lanes == 0, up[b - 1] if b else edge, up[b])
                    after = jnp.where(lanes == 127, down[b + 1] if b < NB - 1 else edge, down[b])
                    beside = ms[f, x, b, rows] + ms[f, x + 2, b, rows] + prev + after
                    spread = cells[b] + kappa[x * NB + b] * (beside - 4.0 * cells[b])
                    high, low = split(spread)
                    columns = slice(half * NYC + b * 128, half * NYC + b * 128 + 128)
                    xs[pair, start:start + keep_rows, columns] = high[0:keep_rows]
                    xs[pair, 64 + start:64 + start + keep_rows, columns] = low[0:keep_rows]
                    xs[pair, 128 + start:128 + start + keep_rows, columns] = high[0:keep_rows]

    def advance(f, carry):
        @pl.when(f + AHEAD < NF)
        def _():
            send_halo(f + AHEAD)

        @pl.when(has_left)
        def _():
            halo(f, 1).wait_recv()

        @pl.when(has_right)
        def _():
            halo(f, 0).wait_recv()

        local = pltpu.roll(outer[...], lax.rem(256 - 2 * NXC * f, 128), axis=1)
        for pair in range(NXC // 2):
            stencil(f, pair, local)
            mixed = jnp.dot(mc[f], xs[pair], preferred_element_type=F32)
            mx[f, 2 * pair] = mixed[0:LP, 0:NYC]
            mx[f, 2 * pair + 1] = mixed[0:LP, NYC:]

        @pl.when(child)
        def _():
            for i in range(4):
                total = mx[f, 3 * i, 0:NL] * nudge[3 * i:3 * i + 1, :]
                for a in range(1, 3):
                    total = total + mx[f, 3 * i + a, 0:NL] * nudge[3 * i + a:3 * i + a + 1, :]
                keep(lhs, i, total)

        @pl.when(parent)
        def _():
            for i in range(4):
                keep(lhs, i, mx[f, nest_x[0] + i, 0:NL])

        picked = jnp.dot(lhs[...], wsel[...], preferred_element_type=F32)
        for i in range(4):
            pay[f, i, 0:NL] = picked[i * 64:i * 64 + NL]
        feedback(f).start()

        @pl.when(f == 0)
        def _():
            vouched(1, (4, 5))
            vouch(2, (4, 5))
            for d in range(1, NTY):
                obs1(d).wait_recv()
            ob[ty] = oa[pl.ds(pl.multiple_of(ty * NTX, NTX), NTX), :]
            for s in range(NTY):
                oc[:, s * SLOTS:(s + 1) * SLOTS] = ob[s, :, 0:SLOTS]
            for d in range(1, NYA):
                obs2(d).start()

        @pl.when(f == 2)
        def _():
            vouched(2, (4, 5))
            for d in range(1, NYA):
                obs2(d).wait_recv()
            own = pl.ds(pl.multiple_of(ya * NZA, NZA), NZA)
            od[own, :] = oc[own, :]
            for z in range(NZA):
                oe[z, 0:NYA] = od[pl.ds(z, NYA, stride=NZA), :]
            for d in range(1, NZA):
                obs3(d).start()

        return carry

    lax.fori_loop(0, NF, advance, 0)

    take = jnp.where(child, 1.0 / 9.0, 1.0)
    give = jnp.where(child, 0.0, 1.0)

    def finish(f, carry):
        feedback(f).wait_recv()
        for i in range(4):
            keep(dlt, i, got[f, i, 0:NL] * take - pay[f, i, 0:NL] * give)
        laid = jnp.dot(dlt[...], wback[...], preferred_element_type=F32)
        for i in range(4):
            cu[i, 0:NL] = laid[i * 64:i * 64 + NL]
        for x in range(NXC):
            p = x - nest_x[0]
            index = jnp.where(child, x // 3, jnp.where((p >= 0) & (p < 4), p, 4))
            done = mx[f, x, 0:NL] + cu[index, 0:NL]
            for b in range(NB):
                raw[f, pl.ds(x * NB + b, NL, stride=STEP), :] = done[:, b * 128:(b + 1) * 128]
        leave(f).start()
        return carry

    def leave(f):
        return pltpu.make_async_copy(raw.at[f], out.at[f], out_sem.at[f])

    lax.fori_loop(0, NF, finish, 0)

    for d in range(1, NZA):
        obs3(d).wait_recv()
    og[za] = oe[za]
    for z in range(NZA):
        packed[z * 8:(z + 1) * 8, :] = og[z]
    leave_obs = pltpu.make_async_copy(packed, obs_out, out_sem.at[NF])
    leave_obs.start()

    for d in range(1, NTY):
        obs1(d).wait_send()
    for d in range(1, NYA):
        obs2(d).wait_send()
    for d in range(1, NZA):
        obs3(d).wait_send()

    @pl.when(has_left)
    def _():
        for f in range(NF):
            halo(f, 0).wait_send()

    @pl.when(has_right)
    def _():
        for f in range(NF):
            halo(f, 1).wait_send()

    @pl.when(has_down)
    def _():
        yedge(0).wait_send()

    @pl.when(has_up)
    def _():
        yedge(1).wait_send()

    for f in range(NF):
        feedback(f).wait_send()
        leave(f).wait()
    leave_obs.wait()


def scatter_kernel(
    vals_in, cells_in, counts_in, start_in, mask_in,
    out, vals, cells, counts, start, mask, terms, wide, index, add0, add1, in_sem, out_sem,
):
    fetches = [
        pltpu.make_async_copy(source, target, in_sem.at[i])
        for i, (source, target) in enumerate(
            [(vals_in, vals), (cells_in, cells), (counts_in, counts), (mask_in, mask), (cells_in, index), (start_in, start)]
        )
    ]
    for fetch in fetches:
        fetch.start()
    add0[...] = jnp.zeros_like(add0)
    add1[...] = jnp.zeros_like(add1)
    for fetch in fetches[:5]:
        fetch.wait()
    for r in range(2 * STEP):
        wide[r:r + 1, :] = mask[r % STEP].astype(F32)
    slot = lax.broadcasted_iota(jnp.int32, (SLOTS, 128), 0)
    lane = lax.broadcasted_iota(jnp.int32, (SLOTS, 128), 1)
    lanes = jnp.where(slot < counts[...], cells[...] & 127, -1)
    turned = vals[...].T
    for s in range(NTY * NTX):
        t, y, z = s // NTX, s % NTX // NZA, s % NZA
        value = turned[t * SLOTS:(t + 1) * SLOTS, z * 8 + y:z * 8 + y + 1]
        terms[s * SLOTS:(s + 1) * SLOTS, :] = jnp.where(lane == lanes[:, s:s + 1], value, 0.0)

    def source(i, carry):
        for u in range(4):
            s = i * 4 + u
            for k in range(SLOTS):
                row = pl.ds(lax.shift_right_logical(index[k, s], 7), 1)
                ref = add1 if k % 2 else add0
                ref[row, :] = ref[row, :] + terms[pl.ds(s * SLOTS + k, 1), :]
        return carry

    lax.fori_loop(0, NTY * NTX // 4, source, 0)
    fetches[5].wait()

    def leave(f):
        rows = pl.ds(f * ROWS, ROWS)
        return pltpu.make_async_copy(add0.at[rows], out.at[rows], out_sem.at[f])

    for f in range(NF):
        def masked(i, carry):
            rows = pl.ds(pl.multiple_of(f * ROWS + i * 2 * STEP, 8), 2 * STEP)
            add0[rows, :] = wide[...] * (start[rows, :] + add0[rows, :] + add1[rows, :])
            return carry

        lax.fori_loop(0, ROWS // (2 * STEP), masked, 0)
        leave(f).start()
    for f in range(NF):
        leave(f).wait()


HBM = pl.BlockSpec(memory_space=pltpu.HBM)
DMA = pltpu.SemaphoreType.DMA


def local(
    adjoint_state, land_mask, diffusivity, mixing, nudging, nest_x, nest_y, obs_forcing, obs_cell, obs_count
):
    state = adjoint_state.reshape(NF, ROWS, 128)
    mask = land_mask.reshape(STEP, 1, 128)
    kappa = diffusivity.reshape(STEP, 1, 128)
    cells = jnp.transpose(obs_cell[0, :, :, 0])
    counts = obs_count[0, :, 0].reshape(1, -1)
    scratch = [
        pltpu.SMEM((1,), jnp.int32),
        pltpu.SMEM((1,), jnp.int32),
        pltpu.VMEM((STEP, 1, 128), jnp.int32),
        pltpu.VMEM((STEP, 1, 128), F32),
        pltpu.VMEM((NXC, NYC), F32),
        pltpu.VMEM((NF, NL, 1, NL), F32),
        pltpu.VMEM((SLOTS, 128), F32),
        pltpu.VMEM((NZA * 8, 128), F32),
        pltpu.VMEM((NF, ROWS, 128), F32),
        pltpu.VMEM((NF, NXC + 2, NB, LP, 128), F32),
        pltpu.VMEM((NXC // 2, 192, 2 * NYC), BF16),
        pltpu.VMEM((NF, 64, 192), BF16),
        pltpu.VMEM((NF, NXC, LP, NYC), F32),
        pltpu.VMEM((2 * NYC, 128), BF16),
        pltpu.VMEM((256, NYC), BF16),
        pltpu.VMEM((256, 2 * NYC), BF16),
        pltpu.VMEM((NF, 4, LP, 128), F32),
        pltpu.VMEM((NF, 4, LP, 128), F32),
        pltpu.VMEM((256, 256), BF16),
        pltpu.VMEM((5, LP, NYC), F32),
        pltpu.VMEM((LP, 128), F32),
        pltpu.VMEM((2, LP, 128), F32),
        pltpu.VMEM((LP, 128), F32),
        pltpu.VMEM((128, 128), F32),
        pltpu.VMEM((NTY, NTX, 128), F32),
        pltpu.VMEM((NTX, 128), F32),
        pltpu.VMEM((NTX, 128), F32),
        pltpu.VMEM((NZA, 8, 128), F32),
        pltpu.VMEM((NZA, 8, 128), F32),
        DMA((NF,)), DMA((2, NF)), DMA((2, NF)), DMA((2,)), DMA((2,)), DMA((NF,)), DMA((NF,)),
        DMA((NTY - 1,)), DMA((NTY - 1,)), DMA((NYA - 1,)), DMA((NYA - 1,)), DMA((NZA - 1,)), DMA((NZA - 1,)),
        DMA((7,)), pltpu.SemaphoreType.REGULAR((3, 6)), DMA((NF + 1,)),
    ]
    partial, arrived = pl.pallas_call(
        exchange_kernel,
        out_shape=(
            jax.ShapeDtypeStruct((NF, ROWS, 128), F32),
            jax.ShapeDtypeStruct((NZA * 8, 128), F32),
        ),
        in_specs=[HBM] * 8,
        out_specs=(HBM, HBM),
        scratch_shapes=scratch,
        compiler_params=pltpu.CompilerParams(
            collective_id=0, has_side_effects=True, vmem_limit_bytes=VMEM_BYTES
        ),
        name="exchange",
    )(nest_x, nest_y, state, mask, kappa, nudging, mixing.reshape(NF, NL, 1, NL), obs_forcing[0, 0])
    total = NF * ROWS
    result = pl.pallas_call(
        scatter_kernel,
        out_shape=jax.ShapeDtypeStruct((total, 128), F32),
        in_specs=[HBM] * 5,
        out_specs=HBM,
        scratch_shapes=[
            pltpu.VMEM((NZA * 8, 128), F32), pltpu.VMEM((SLOTS, NTY * NTX), jnp.int32),
            pltpu.VMEM((1, NTY * NTX), jnp.int32), pltpu.VMEM((total, 128), F32), pltpu.VMEM((STEP, 1, 128), jnp.int32),
            pltpu.VMEM((NTY * NTX * SLOTS, 128), F32), pltpu.VMEM((2 * STEP, 128), F32),
            pltpu.SMEM((SLOTS, NTY * NTX), jnp.int32),
            pltpu.VMEM((total, 128), F32), pltpu.VMEM((total, 128), F32), DMA((6,)), DMA((NF,)),
        ],
        compiler_params=pltpu.CompilerParams(vmem_limit_bytes=VMEM_BYTES),
        name="scatter",
    )(arrived, cells, counts, partial.reshape(total, 128), mask)
    return result.reshape(1, NF, NL, NXC, NYC)


def solution(mesh):
    in_specs = (
        P("grp", None, None, "tx", "ty"),
        P("grp", "tx", "ty"),
        P("grp", "tx", "ty"),
        P("grp", None, None, None),
        P("tx", "ty"),
        P(("ty", "tx")),
        P(("ty", "tx")),
        P("grp", ("ty", "tx"), None, None),
        P("grp", None, None, ("ty", "tx")),
        P("grp", None, ("ty", "tx")),
    )
    out_specs = P("grp", None, None, "tx", "ty")
    return jax.shard_map(local, mesh=mesh, in_specs=in_specs, out_specs=out_specs, check_vma=False)
```

```python
import functools

import jax
import jax.numpy as jnp
from jax import lax
from jax.experimental import pallas as pl
from jax.experimental.pallas import tpu as pltpu
from jax.sharding import PartitionSpec as P

MESH = pl.DeviceIdType.MESH
F32 = jnp.float32
BF16 = jnp.bfloat16
NF, NL, NXC, NYC = 5, 50, 12, 384
LP = 56
NB = NYC // 128
ROWS = NL * NXC * NB
STEP = NXC * NB
NTY, NTX, NYA, NZA = 4, 32, 4, 8
SLOTS = 16
AHEAD = 2
VMEM_BYTES = 63 * 2**20


def split(value):
    high = value.astype(BF16)
    low = (value - high.astype(F32)).astype(BF16)
    return high, low


def exchange_kernel(
    nest_x_in, nest_y_in, state, mask_in, kappa_in, nudge_in, mix_in, obs_in,
    out, obs_out,
    nest_x, nest_y, mask, kappa, nudge, mix, obs, packed,
    raw, ms, xs, mc, mx, wsel, wback, lhs, pay, got, dlt, cu,
    ycols, yhalo, outer, oa, ob, oc, od, oe, og,
    in_sem, hs_sem, hr_sem, ys_sem, yr_sem, gs_sem, gr_sem,
    os1, or1, os2, or2, os3, or3, small_sem, far_sem, out_sem,
):
    grp = lax.axis_index("grp")
    ty = lax.axis_index("ty")
    tx = lax.axis_index("tx")
    ya, za = tx // NZA, tx % NZA
    child = grp == 0
    parent = grp == 1

    def dev(g=None, y=None, x=None):
        return (grp if g is None else g, ty if y is None else y, tx if x is None else x)

    def fetch(f):
        return pltpu.make_async_copy(state.at[f], raw.at[f], in_sem.at[f])

    smalls = [
        pltpu.make_async_copy(source, target, small_sem.at[i])
        for i, (source, target) in enumerate(
            [(obs_in, obs), (mask_in, mask), (mix_in, mix), (nest_x_in, nest_x), (nest_y_in, nest_y),
             (kappa_in, kappa), (nudge_in, nudge)]
        )
    ]
    smalls[0].start()
    smalls[1].start()
    for f in range(NF):
        fetch(f).start()
    for copy in smalls[2:]:
        copy.start()

    barrier = pltpu.get_barrier_semaphore()

    def greet(target):
        pl.semaphore_signal(barrier, inc=1, device_id=target, device_id_type=MESH)

    has_left, has_right = tx > 0, tx < NTX - 1
    has_down, has_up = ty > 0, ty < NTY - 1
    ring = (
        dev(y=(ty + 1) % NTY), dev(y=(ty + 3) % NTY),
        dev(x=((ya + 1) % NYA) * NZA + za), dev(x=((ya + 3) % NYA) * NZA + za),
        dev(x=ya * NZA + (za + 1) % NZA), dev(x=ya * NZA + (za + 7) % NZA),
    )
    greet(dev(g=1 - grp))
    for device in ring:
        greet(device)
    wrap_left = (za == 0) & has_left
    wrap_right = (za == NZA - 1) & has_right

    @pl.when(wrap_left)
    def _():
        greet(dev(x=tx - 1))

    @pl.when(wrap_right)
    def _():
        greet(dev(x=tx + 1))

    def vouch(stage, sides):
        for side in sides:
            pl.semaphore_signal(
                far_sem.at[stage, side], inc=1, device_id=ring[side], device_id_type=MESH
            )

    def vouched(stage, sides):
        for side in sides:
            pl.semaphore_wait(far_sem.at[stage, side], 1)

    for copy in smalls:
        copy.wait()
    oa[:, 0:SLOTS] = obs[...].T
    lane = lax.broadcasted_iota(jnp.int32, (NL, 128), 1)
    scale = jnp.where(child, 3, 1)
    off = jnp.where(child, 0, nest_y[0])

    def selection(shape, ydim):
        d = lax.broadcasted_iota(jnp.int32, shape, ydim)
        d = d - scale * lax.broadcasted_iota(jnp.int32, shape, 1 - ydim) - off
        return jnp.where((d >= 0) & (d < scale), 1.0, 0.0).astype(BF16)

    wsel[0:NYC] = selection((NYC, 128), 0)
    wsel[NYC:] = wsel[0:NYC]
    wback[0:128] = selection((128, NYC), 1)
    wback[128:] = wback[0:128]
    mc[...] = jnp.zeros_like(mc)
    xs[...] = jnp.zeros_like(xs)
    for f in range(NF):
        high, low = split(mix[f, :, 0, :])
        mc[f, 0:NL, 0:NL] = high
        mc[f, 0:NL, 64:64 + NL] = high
        mc[f, 0:NL, 128:128 + NL] = low
    cu[4] = jnp.zeros(cu.shape[1:], F32)

    @pl.when(tx == 0)
    def _():
        for f in range(NF):
            ms[f, 0] = jnp.zeros(ms.shape[2:], F32)

    @pl.when(tx == NTX - 1)
    def _():
        for f in range(NF):
            ms[f, NXC + 1] = jnp.zeros(ms.shape[2:], F32)

    @pl.when(ty == 0)
    def _():
        yhalo[0] = jnp.zeros(yhalo.shape[1:], F32)

    @pl.when(ty == NTY - 1)
    def _():
        yhalo[1] = jnp.zeros(yhalo.shape[1:], F32)

    def obs1(d):
        peer = (ty + d) % NTY
        return pltpu.make_async_remote_copy(
            oa.at[pl.ds(pl.multiple_of(peer * NTX, NTX), NTX)], ob.at[ty], os1.at[d - 1], or1.at[d - 1],
            device_id=dev(y=peer), device_id_type=MESH,
        )

    def obs2(d):
        peer = (ya + d) % NYA
        return pltpu.make_async_remote_copy(
            oc.at[pl.ds(pl.multiple_of(peer * NZA, NZA), NZA)],
            od.at[pl.ds(pl.multiple_of(ya * NZA, NZA), NZA)], os2.at[d - 1], or2.at[d - 1],
            device_id=dev(x=peer * NZA + za), device_id_type=MESH,
        )

    def obs3(d):
        peer = (za + d) % NZA
        return pltpu.make_async_remote_copy(
            oe.at[peer], og.at[za], os3.at[d - 1], or3.at[d - 1],
            device_id=dev(x=ya * NZA + peer), device_id_type=MESH,
        )

    def halo(f, side):
        source, target, x = (1, NXC + 1, tx - 1) if side == 0 else (NXC, 0, tx + 1)
        return pltpu.make_async_remote_copy(
            ms.at[f, source, :, pl.ds(0, NL)], ms.at[f, target, :, pl.ds(0, NL)], hs_sem.at[side, f], hr_sem.at[side, f],
            device_id=dev(x=x), device_id_type=MESH,
        )

    def send_halo(f):
        @pl.when(has_left)
        def _():
            halo(f, 0).start()

        @pl.when(has_right)
        def _():
            halo(f, 1).start()

    def meet():
        pl.semaphore_wait(barrier, 1 + len(ring) + jnp.where(wrap_left | wrap_right, 1, 0))
        vouch(0, range(6))

    @pl.when(za != 0)
    def _():
        meet()

    def planes(f, carry):
        fetch(f).wait()
        edge = jnp.zeros((NL, 128), F32)
        for x in range(NXC):
            value = []
            for b in range(NB):
                r = x * NB + b
                value.append(raw[f, pl.ds(r, NL, stride=STEP), :] * mask[r].astype(F32))
                ms[f, x + 1, b, 0:NL] = value[b]
            pair = jnp.where(lane < 64, value[0], value[NB - 1])
            here = (lane == 2 * x) | (lane == (2 * x - 1) % 128)
            edge = jnp.where(here, pltpu.roll(pair, 2 * x, axis=1) if x else pair, edge)

        @pl.when((f < AHEAD) & (za != 0))
        def _():
            send_halo(f)

        turned = pltpu.roll(edge, 2 * NXC * f, axis=1)
        return jnp.where(((lane + 1 - 2 * NXC * f) & 127) < 2 * NXC, turned, carry)

    ycols[0:NL] = lax.fori_loop(0, NF, planes, jnp.zeros((NL, 128), F32))

    def yedge(side):
        return pltpu.make_async_remote_copy(
            ycols.at[pl.ds(0, NL)], yhalo.at[1 - side, pl.ds(0, NL)], ys_sem.at[side], yr_sem.at[side],
            device_id=dev(y=ty - 1 if side == 0 else ty + 1), device_id_type=MESH,
        )

    @pl.when(za == 0)
    def _():
        meet()
        for f in range(AHEAD):
            send_halo(f)

    @pl.when(has_down)
    def _():
        yedge(0).start()

    @pl.when(has_up)
    def _():
        yedge(1).start()

    vouched(0, range(6))
    vouch(1, (4, 5))
    for d in range(1, NTY):
        obs1(d).start()

    @pl.when(has_down)
    def _():
        yedge(1).wait_recv()

    @pl.when(has_up)
    def _():
        yedge(0).wait_recv()

    even = (lane & 1) == 0
    outer[0:NL] = jnp.where(
        even, pltpu.roll(yhalo[0, 0:NL], 1, axis=1), pltpu.roll(yhalo[1, 0:NL], 127, axis=1)
    )

    def feedback(f):
        return pltpu.make_async_remote_copy(
            pay.at[f, :, pl.ds(0, NL)], got.at[f, :, pl.ds(0, NL)], gs_sem.at[f], gr_sem.at[f],
            device_id=dev(g=1 - grp), device_id_type=MESH,
        )

    def keep(ref, i, value):
        high, low = split(value)
        width = value.shape[1]
        ref[i * 64:i * 64 + NL, 0:width] = high
        ref[i * 64:i * 64 + NL, width:2 * width] = low

    lane16 = lax.broadcasted_iota(jnp.int32, (16, 128), 1)

    def stencil(f, pair, local):
        for start, size in ((0, 16), (16, 16), (32, 16), (48, 8)):
            rows = slice(start, start + size)
            keep_rows = min(size, NL - start)
            lanes = lane16[0:size]
            for half in range(2):
                x = 2 * pair + half
                cells = [ms[f, x + 1, b, rows] for b in range(NB)]
                edge = pltpu.roll(local[rows], 128 - 2 * x, axis=1) if x else local[rows]
                up = [pltpu.roll(c, 1, axis=1) for c in cells]
                down = [pltpu.roll(c, 127, axis=1) for c in cells]
                for b in range(NB):
                    prev = jnp.where(lanes == 0, up[b - 1] if b else edge, up[b])
                    after = jnp.where(lanes == 127, down[b + 1] if b < NB - 1 else edge, down[b])
                    beside = ms[f, x, b, rows] + ms[f, x + 2, b, rows] + prev + after
                    spread = cells[b] + kappa[x * NB + b] * (beside - 4.0 * cells[b])
                    high, low = split(spread)
                    columns = slice(half * NYC + b * 128, half * NYC + b * 128 + 128)
                    xs[pair, start:start + keep_rows, columns] = high[0:keep_rows]
                    xs[pair, 64 + start:64 + start + keep_rows, columns] = low[0:keep_rows]
                    xs[pair, 128 + start:128 + start + keep_rows, columns] = high[0:keep_rows]

    def advance(f, carry):
        @pl.when(f + AHEAD < NF)
        def _():
            send_halo(f + AHEAD)

        @pl.when(has_left)
        def _():
            halo(f, 1).wait_recv()

        @pl.when(has_right)
        def _():
            halo(f, 0).wait_recv()

        local = pltpu.roll(outer[...], lax.rem(256 - 2 * NXC * f, 128), axis=1)
        for pair in range(NXC // 2):
            stencil(f, pair, local)
            mixed = jnp.dot(mc[f], xs[pair], preferred_element_type=F32)
            mx[f, 2 * pair] = mixed[0:LP, 0:NYC]
            mx[f, 2 * pair + 1] = mixed[0:LP, NYC:]

        @pl.when(child)
        def _():
            for i in range(4):
                total = mx[f, 3 * i, 0:NL] * nudge[3 * i:3 * i + 1, :]
                for a in range(1, 3):
                    total = total + mx[f, 3 * i + a, 0:NL] * nudge[3 * i + a:3 * i + a + 1, :]
                keep(lhs, i, total)

        @pl.when(parent)
        def _():
            for i in range(4):
                keep(lhs, i, mx[f, nest_x[0] + i, 0:NL])

        picked = jnp.dot(lhs[...], wsel[...], preferred_element_type=F32)
        for i in range(4):
            pay[f, i, 0:NL] = picked[i * 64:i * 64 + NL]
        feedback(f).start()

        @pl.when(f == 0)
        def _():
            vouched(1, (4, 5))
            vouch(2, (4, 5))
            for d in range(1, NTY):
                obs1(d).wait_recv()
            ob[ty] = oa[pl.ds(pl.multiple_of(ty * NTX, NTX), NTX), :]
            for s in range(NTY):
                oc[:, s * SLOTS:(s + 1) * SLOTS] = ob[s, :, 0:SLOTS]
            for d in range(1, NYA):
                obs2(d).start()

        @pl.when(f == 2)
        def _():
            vouched(2, (4, 5))
            for d in range(1, NYA):
                obs2(d).wait_recv()
            own = pl.ds(pl.multiple_of(ya * NZA, NZA), NZA)
            od[own, :] = oc[own, :]
            for z in range(NZA):
                oe[z, 0:NYA] = od[pl.ds(z, NYA, stride=NZA), :]
            for d in range(1, NZA):
                obs3(d).start()

        return carry

    lax.fori_loop(0, NF, advance, 0)

    take = jnp.where(child, 1.0 / 9.0, 1.0)
    give = jnp.where(child, 0.0, 1.0)

    def finish(f, carry):
        feedback(f).wait_recv()
        for i in range(4):
            keep(dlt, i, got[f, i, 0:NL] * take - pay[f, i, 0:NL] * give)
        laid = jnp.dot(dlt[...], wback[...], preferred_element_type=F32)
        for i in range(4):
            cu[i, 0:NL] = laid[i * 64:i * 64 + NL]
        for x in range(NXC):
            p = x - nest_x[0]
            index = jnp.where(child, x // 3, jnp.where((p >= 0) & (p < 4), p, 4))
            done = mx[f, x, 0:NL] + cu[index, 0:NL]
            for b in range(NB):
                raw[f, pl.ds(x * NB + b, NL, stride=STEP), :] = done[:, b * 128:(b + 1) * 128]
        leave(f).start()
        return carry

    def leave(f):
        return pltpu.make_async_copy(raw.at[f], out.at[f], out_sem.at[f])

    lax.fori_loop(0, NF, finish, 0)

    for d in range(1, NZA):
        obs3(d).wait_recv()
    og[za] = oe[za]
    for z in range(NZA):
        packed[z * 8:(z + 1) * 8, :] = og[z]
    leave_obs = pltpu.make_async_copy(packed, obs_out, out_sem.at[NF])
    leave_obs.start()

    for d in range(1, NTY):
        obs1(d).wait_send()
    for d in range(1, NYA):
        obs2(d).wait_send()
    for d in range(1, NZA):
        obs3(d).wait_send()

    @pl.when(has_left)
    def _():
        for f in range(NF):
            halo(f, 0).wait_send()

    @pl.when(has_right)
    def _():
        for f in range(NF):
            halo(f, 1).wait_send()

    @pl.when(has_down)
    def _():
        yedge(0).wait_send()

    @pl.when(has_up)
    def _():
        yedge(1).wait_send()

    for f in range(NF):
        feedback(f).wait_send()
        leave(f).wait()
    leave_obs.wait()


def scatter_kernel(
    vals_in, cells_in, counts_in, start_in, mask_in,
    out, vals, cells, counts, start, mask, terms, wide, index, add0, add1, in_sem, out_sem,
):
    fetches = [
        pltpu.make_async_copy(source, target, in_sem.at[i])
        for i, (source, target) in enumerate(
            [(vals_in, vals), (cells_in, cells), (counts_in, counts), (mask_in, mask), (cells_in, index), (start_in, start)]
        )
    ]
    for fetch in fetches:
        fetch.start()
    add0[...] = jnp.zeros_like(add0)
    add1[...] = jnp.zeros_like(add1)
    for fetch in fetches[:5]:
        fetch.wait()
    for r in range(2 * STEP):
        wide[r:r + 1, :] = mask[r % STEP].astype(F32)
    slot = lax.broadcasted_iota(jnp.int32, (SLOTS, 128), 0)
    lane = lax.broadcasted_iota(jnp.int32, (SLOTS, 128), 1)
    lanes = jnp.where(slot < counts[...], cells[...] & 127, -1)
    turned = vals[...].T
    for s in range(NTY * NTX):
        t, y, z = s // NTX, s % NTX // NZA, s % NZA
        value = turned[t * SLOTS:(t + 1) * SLOTS, z * 8 + y:z * 8 + y + 1]
        terms[s * SLOTS:(s + 1) * SLOTS, :] = jnp.where(lane == lanes[:, s:s + 1], value, 0.0)

    def source(i, carry):
        for u in range(4):
            s = i * 4 + u
            for k in range(SLOTS):
                row = pl.ds(lax.shift_right_logical(index[k, s], 7), 1)
                ref = add1 if k % 2 else add0
                ref[row, :] = ref[row, :] + terms[pl.ds(s * SLOTS + k, 1), :]
        return carry

    lax.fori_loop(0, NTY * NTX // 4, source, 0)
    fetches[5].wait()

    def leave(f):
        rows = pl.ds(f * ROWS, ROWS)
        return pltpu.make_async_copy(add0.at[rows], out.at[rows], out_sem.at[f])

    for f in range(NF):
        def masked(i, carry):
            rows = pl.ds(pl.multiple_of(f * ROWS + i * 2 * STEP, 8), 2 * STEP)
            add0[rows, :] = wide[...] * (start[rows, :] + add0[rows, :] + add1[rows, :])
            return carry

        lax.fori_loop(0, ROWS // (2 * STEP), masked, 0)
        leave(f).start()
    for f in range(NF):
        leave(f).wait()


HBM = pl.BlockSpec(memory_space=pltpu.HBM)
DMA = pltpu.SemaphoreType.DMA


def local(
    adjoint_state, land_mask, diffusivity, mixing, nudging, nest_x, nest_y, obs_forcing, obs_cell, obs_count
):
    state = adjoint_state.reshape(NF, ROWS, 128)
    mask = land_mask.reshape(STEP, 1, 128)
    kappa = diffusivity.reshape(STEP, 1, 128)
    cells = jnp.transpose(obs_cell[0, :, :, 0])
    counts = obs_count[0, :, 0].reshape(1, -1)
    scratch = [
        pltpu.SMEM((1,), jnp.int32),
        pltpu.SMEM((1,), jnp.int32),
        pltpu.VMEM((STEP, 1, 128), jnp.int32),
        pltpu.VMEM((STEP, 1, 128), F32),
        pltpu.VMEM((NXC, NYC), F32),
        pltpu.VMEM((NF, NL, 1, NL), F32),
        pltpu.VMEM((SLOTS, 128), F32),
        pltpu.VMEM((NZA * 8, 128), F32),
        pltpu.VMEM((NF + 1, ROWS, 128), F32),
        pltpu.VMEM((NF, NXC + 2, NB, LP, 128), F32),
        pltpu.VMEM((NXC // 2, 192, 2 * NYC), BF16),
        pltpu.VMEM((NF, 64, 192), BF16),
        pltpu.VMEM((NF, NXC, LP, NYC), F32),
        pltpu.VMEM((2 * NYC, 128), BF16),
        pltpu.VMEM((256, NYC), BF16),
        pltpu.VMEM((256, 2 * NYC), BF16),
        pltpu.VMEM((NF, 4, LP, 128), F32),
        pltpu.VMEM((NF, 4, LP, 128), F32),
        pltpu.VMEM((256, 256), BF16),
        pltpu.VMEM((5, LP, NYC), F32),
        pltpu.VMEM((LP, 128), F32),
        pltpu.VMEM((2, LP, 128), F32),
        pltpu.VMEM((LP, 128), F32),
        pltpu.VMEM((128, 128), F32),
        pltpu.VMEM((NTY, NTX, 128), F32),
        pltpu.VMEM((NTX, 128), F32),
        pltpu.VMEM((2 * NTX, 128), F32),
        pltpu.VMEM((NZA, 8, 128), F32),
        pltpu.VMEM((NZA, 8, 128), F32),
        DMA((NF,)), DMA((2, NF)), DMA((2, NF)), DMA((2,)), DMA((2,)), DMA((NF,)), DMA((NF,)),
        DMA((NTY - 1,)), DMA((NTY - 1,)), DMA((NYA - 1,)), DMA((NYA - 1,)), DMA((NZA - 1,)), DMA((NZA - 1,)),
        DMA((7,)), pltpu.SemaphoreType.REGULAR((3, 6)), DMA((NF + 1,)),
    ]
    partial, arrived = pl.pallas_call(
        exchange_kernel,
        out_shape=(
            jax.ShapeDtypeStruct((NF, ROWS, 128), F32),
            jax.ShapeDtypeStruct((NZA * 8, 128), F32),
        ),
        in_specs=[HBM] * 8,
        out_specs=(HBM, HBM),
        scratch_shapes=scratch,
        compiler_params=pltpu.CompilerParams(
            collective_id=0, has_side_effects=True, vmem_limit_bytes=VMEM_BYTES
        ),
        name="exchange",
    )(nest_x, nest_y, state, mask, kappa, nudging, mixing.reshape(NF, NL, 1, NL), obs_forcing[0, 0])
    total = NF * ROWS
    result = pl.pallas_call(
        scatter_kernel,
        out_shape=jax.ShapeDtypeStruct((total, 128), F32),
        in_specs=[HBM] * 5,
        out_specs=HBM,
        scratch_shapes=[
            pltpu.VMEM((NZA * 8, 128), F32), pltpu.VMEM((SLOTS, NTY * NTX), jnp.int32),
            pltpu.VMEM((1, NTY * NTX), jnp.int32), pltpu.VMEM((total, 128), F32), pltpu.VMEM((STEP, 1, 128), jnp.int32),
            pltpu.VMEM((NTY * NTX * SLOTS, 128), F32), pltpu.VMEM((2 * STEP, 128), F32),
            pltpu.SMEM((SLOTS, NTY * NTX), jnp.int32),
            pltpu.VMEM((total, 128), F32), pltpu.VMEM((total, 128), F32), DMA((6,)), DMA((NF,)),
        ],
        compiler_params=pltpu.CompilerParams(vmem_limit_bytes=VMEM_BYTES),
        name="scatter",
    )(arrived, cells, counts, partial.reshape(total, 128), mask)
    return result.reshape(1, NF, NL, NXC, NYC)


def solution(mesh):
    in_specs = (
        P("grp", None, None, "tx", "ty"),
        P("grp", "tx", "ty"),
        P("grp", "tx", "ty"),
        P("grp", None, None, None),
        P("tx", "ty"),
        P(("ty", "tx")),
        P(("ty", "tx")),
        P("grp", ("ty", "tx"), None, None),
        P("grp", None, None, ("ty", "tx")),
        P("grp", None, ("ty", "tx")),
    )
    out_specs = P("grp", None, None, "tx", "ty")
    return jax.shard_map(local, mesh=mesh, in_specs=in_specs, out_specs=out_specs, check_vma=False)
```
